256 devices in a mesh: span: 8 (over y_hi, x), wall: 32 (over y_lo, z, core).
Axes of the slice: x: 4, y: 4 (y_hi: 2, y_lo: 2; y = y_hi * 2 + y_lo), z: 8, core: 2. Of those that a mesh axis runs over, the one named last changes fastest.
Arguments:
- forcing: bfloat16 [2, 5, 4, 128, 128, 128], P(None, None, None, 'span', 'wall'), may hold values from -6 to 6
- span_factor: float32 [2, 5, 128], replicated, may hold values from -1 to 1
- pivot_inverse: bfloat16 [2, 5, 5, 128, 128, 128], P(None, None, None, 'span', 'wall'), may hold values from -0.046875 to 0.046875
- step_lower: bfloat16 [2, 5, 5, 128, 128, 128], P(None, None, None, 'span', 'wall'), may hold values from -1 to 1
- step_upper: bfloat16 [2, 5, 5, 128, 128, 128], P(None, None, None, 'span', 'wall'), may hold values from -1 to 1
Outputs:
- response: float32 [2, 5, 4, 128, 128, 128], P(None, None, None, 'span', 'wall')
The draws below stay inside these ranges and needn't reach their ends.
All inputs are finite; a program needn't handle non-finite values.
Results may differ from the reference program's by a relative error of at most 0.0003.
Values may be sent and summed in bfloat16 or wider, within the bound.
A program may use at most 128 MiB of HBM per device.

```python
import math
import jax
import jax.numpy as jnp
from jax import lax

FIELDS = 5
NZ = 128
NX = 128
COLS = 4
WALL_NORMAL_ROWS = 128


def decay_block(key):
    shape = (2, FIELDS, FIELDS, NZ, WALL_NORMAL_ROWS, NX)
    random_keys = jax.random.split(key, 7)
    slow_share = 0.5
    lane = (FIELDS, NZ, 1, NX)
    pick = jax.random.uniform(random_keys[0], lane)
    slow_rate = jax.random.uniform(random_keys[1], lane, minval=0.2, maxval=1.0) * (0.6 / WALL_NORMAL_ROWS)
    fast_rate = math.log(10.0) / jax.random.uniform(random_keys[2], lane, minval=30.0, maxval=50.0)
    growth_factor = jnp.where(pick < slow_share, slow_rate, fast_rate)
    height = jnp.arange(WALL_NORMAL_ROWS, dtype=jnp.float32).reshape(1, 1, WALL_NORMAL_ROWS, 1)
    growth_factor = growth_factor * (1.0 + height / WALL_NORMAL_ROWS)
    pulse_selection = jax.random.uniform(random_keys[3], (1, 1, WALL_NORMAL_ROWS, 1))
    pulse_length = jax.random.uniform(random_keys[4], (1, 1, WALL_NORMAL_ROWS, 1), minval=0.5, maxval=0.8)
    pulse_group = jnp.where(pulse_selection < 3.0 / WALL_NORMAL_ROWS, pulse_length, 1.0)
    forcing_amplitude = jnp.exp(-growth_factor - 0.01) * pulse_group
    phase = jax.random.uniform(random_keys[5], (FIELDS, NZ, WALL_NORMAL_ROWS, NX), minval=-math.pi, maxval=math.pi)
    coupling = jnp.clip(0.045 * jax.random.normal(random_keys[6], shape), -0.2, 0.2)
    unit = jnp.eye(FIELDS, dtype=jnp.float32).reshape(1, FIELDS, FIELDS, 1, 1, 1)
    diagonal = jnp.stack([forcing_amplitude * jnp.cos(phase), forcing_amplitude * jnp.sin(phase)])
    return coupling * (1.0 - unit) + diagonal[:, :, None] * unit


def draw_step_lower(key, part):
    return decay_block(jax.random.fold_in(key, 11)).astype(jnp.bfloat16)


def draw_step_upper(key, part):
    return decay_block(jax.random.fold_in(key, 29)).astype(jnp.bfloat16)


def block_levels(key, extent, cuts, least, top_value):
    loudness = 1.0
    for position, blocks in cuts:
        draws = jax.random.uniform(jax.random.fold_in(jax.random.fold_in(key, 6), position), (blocks,), jnp.float32, least / len(cuts), top_value / len(cuts))
        loudness = loudness * jnp.repeat(jnp.exp(draws), extent[position] // blocks).reshape((-1,) + (1,) * (len(extent) - 1 - position))
    return loudness


def noise(rng, dims, scale, most, cuts=(), kind=jnp.bfloat16):
    entries = jax.random.normal(rng, dims, jnp.float32) * scale
    if len(cuts) > 0:
        entries = block_levels(rng, dims, cuts, -0.22, 0.18) * entries
    return jnp.clip(entries, min=-most, max=most).astype(kind)


def setup_inputs(seed: int = 0) -> dict:
    splits = jax.random.split(jax.random.key(seed), 6)
    forcing = noise(splits[0], (2, FIELDS, COLS, NZ, WALL_NORMAL_ROWS, NX), 1.0, 6.0, ((3, 8), (4, 32)))
    span_factor = jnp.clip(jax.random.uniform(splits[1], (2, FIELDS, NZ), jnp.float32, -1.0, 1.0), -1.0, 1.0)
    pivot_inverse = noise(splits[2], (2, FIELDS, FIELDS, NZ, WALL_NORMAL_ROWS, NX), (1.0 / WALL_NORMAL_ROWS), 0.046875, ((3, 8), (4, 32)))
    step_lower = draw_step_lower(jax.random.fold_in(splits[5], 71), 0)
    step_upper = draw_step_upper(jax.random.fold_in(splits[5], 71), 0)
    return {"forcing": forcing, "span_factor": span_factor, "pivot_inverse": pivot_inverse, "step_lower": step_lower, "step_upper": step_upper}


exact_mode = lax.Precision.HIGHEST


def block_vector(matrix, vector):
    real = jnp.einsum("ijzx,jczx->iczx", matrix[0], vector[0], precision=exact_mode) - jnp.einsum("ijzx,jczx->iczx", matrix[1], vector[1], precision=exact_mode)
    imag = jnp.einsum("ijzx,jczx->iczx", matrix[0], vector[1], precision=exact_mode) + jnp.einsum("ijzx,jczx->iczx", matrix[1], vector[0], precision=exact_mode)
    return jnp.stack([real, imag])


def spectral_tables(count):
    modes = jnp.arange(count, dtype=jnp.int32)
    angle = ((modes[:, None] * modes[None, :]) % count).astype(jnp.float32) * (2.0 * math.pi / count)
    return jnp.cos(angle), jnp.sin(angle)


def reference(forcing, span_factor, pivot_inverse, step_lower, step_upper):
    cosine, sine = spectral_tables(NZ)

    def filter_field(inputs):
        field_re, field_im, factor = inputs
        field_re = field_re.astype(jnp.float32)
        field_im = field_im.astype(jnp.float32)
        spec_re = jnp.einsum("kz,qzyx->qkyx", cosine, field_re, precision=exact_mode) + jnp.einsum("kz,qzyx->qkyx", sine, field_im, precision=exact_mode)
        spec_im = jnp.einsum("kz,qzyx->qkyx", cosine, field_im, precision=exact_mode) - jnp.einsum("kz,qzyx->qkyx", sine, field_re, precision=exact_mode)
        factor_re = factor[0][None, :, None, None]
        factor_im = factor[1][None, :, None, None]
        filt_re = factor_re * spec_re - factor_im * spec_im
        filt_im = factor_re * spec_im + factor_im * spec_re
        back_re = (jnp.einsum("kz,qkyx->qzyx", cosine, filt_re, precision=exact_mode) - jnp.einsum("kz,qkyx->qzyx", sine, filt_im, precision=exact_mode)) / NZ
        back_im = (jnp.einsum("kz,qkyx->qzyx", cosine, filt_im, precision=exact_mode) + jnp.einsum("kz,qkyx->qzyx", sine, filt_re, precision=exact_mode)) / NZ
        return jnp.stack([back_re, back_im])

    driving = lax.map(filter_field, (forcing[0], forcing[1], jnp.transpose(span_factor, (1, 0, 2))))
    driving = jnp.transpose(driving, (1, 0, 2, 3, 4, 5))
    heights = jnp.arange(WALL_NORMAL_ROWS, dtype=jnp.int32)

    def forward_step(previous, height):
        pivot = lax.dynamic_index_in_dim(pivot_inverse, height, 4, False).astype(jnp.float32)
        lower = lax.dynamic_index_in_dim(step_lower, height, 4, False).astype(jnp.float32)
        source = lax.dynamic_index_in_dim(driving, height, 4, False)
        current = block_vector(pivot, source) - block_vector(lower, previous)
        return current, current

    start_state = jnp.zeros((2, FIELDS, COLS, NZ, NX), jnp.float32)
    sweep_rows = lax.scan(forward_step, start_state, heights)[1]

    def backward_step(following, inputs):
        height, sweep = inputs
        upper = lax.dynamic_index_in_dim(step_upper, height, 4, False).astype(jnp.float32)
        current = sweep - block_vector(upper, following)
        return current, current

    response_rows = lax.scan(backward_step, start_state, (heights, sweep_rows), reverse=True)[1]
    return jnp.moveaxis(response_rows, 0, 4)
```

```python
import functools
import math

import jax
import jax.numpy as jnp
import numpy as np
from jax import lax
from jax.experimental import pallas as pl
from jax.experimental.pallas import tpu as pltpu
from jax.sharding import PartitionSpec as P

MESH = pl.DeviceIdType.MESH
F = 5
S = 8
K = 16
ROWS = 8
TR = 80
AR = 24
HI = lax.Precision.HIGHEST


def apply(coef, y, vectors):
    out = [None] * len(vectors)
    for j in range(F):
        cr = coef[y, 0, j]
        ci = coef[y, 1, j]
        for n, (vr, vi) in enumerate(vectors):
            xr = vr[j][None]
            xi = vi[j][None]
            re = cr * xr - ci * xi
            im = cr * xi + ci * xr
            out[n] = (re, im) if out[n] is None else (out[n][0] + re, out[n][1] + im)
    return out


def sub(a, b):
    return [(x[0] - y[0], x[1] - y[1]) for x, y in zip(a, b)]


def kernel(
    forcing, factor, table, piv, low, upp, out,
    tmp, send_f, recv_f, part_p, part_l, part_u, pf, lf, uf, pre, tm, a_hi, a_lo,
    send_r, driv, send_t, recv_t, te, send_a, recv_a, send_s, recv_s, src, sw, qb, resp,
    c_send, c_recv, f_send, f_recv, r_send, r_recv, t_send, t_recv, a_send, a_recv, s_send, s_recv,
    o_send, o_recv, loc,
):
    me_s = lax.axis_index("span")
    me_w = lax.axis_index("wall")
    core = lax.rem(me_w, 2)
    chip = me_w // 2
    other = 1 - core
    partner = chip * 2 + other

    def span_peer(o):
        return lax.rem(me_s + o, S)

    def wall_peer(o):
        return lax.rem(chip + o, K)

    barrier = pltpu.get_barrier_semaphore()

    def greet(s, w):
        pl.semaphore_signal(barrier, inc=1, device_id=(s, w), device_id_type=MESH)

    def greet_span(o, carry):
        greet(span_peer(o), me_w)
        greet(span_peer(o), partner)
        return carry

    def greet_wall(o, carry):
        greet(me_s, wall_peer(o) * 2 + core)
        return carry

    lax.fori_loop(1, S, greet_span, 0)
    lax.fori_loop(1, K, greet_wall, 0)
    greet(me_s, partner)

    def regroup(g, carry):
        for col in range(4):
            tmp[pl.ds(col * 64, 64), :] = forcing[g, col].astype(jnp.float32)
        for col in range(4):
            for y in range(4):
                piece = tmp[pl.ds(col * 64 + y, 16, stride=4), :].astype(jnp.bfloat16)
                send_f[col // 2, (col % 2) * 4 + y, lax.rem(g, F), g // F] = piece
        return carry

    lax.fori_loop(0, 2 * F, regroup, 0)

    pl.semaphore_wait(barrier, 2 * S - 1 + K - 1)

    def remote(src_ref, dst_ref, ss, rs, s, w):
        return pltpu.make_async_remote_copy(
            src_ref=src_ref, dst_ref=dst_ref, send_sem=ss, recv_sem=rs,
            device_id=(s, w), device_id_type=MESH,
        )

    def f_copy(ch, o):
        to = span_peer(o)
        return remote(send_f.at[ch, to], recv_f.at[ch, me_s], f_send.at[ch, to], f_recv.at[ch, me_s], to, me_w)

    def f_wait(ch, o):
        frm = span_peer(o)
        return remote(send_f.at[ch, frm], recv_f.at[ch, frm], f_send.at[ch, frm], f_recv.at[ch, frm], frm, me_w)

    def f_local(ch):
        return pltpu.make_async_copy(send_f.at[ch, me_s], recv_f.at[ch, me_s], loc.at[0, ch])

    def c_copy(n, ref, part):
        return remote(ref.at[:, pl.ds(other * 32, 32), :], part, c_send.at[n], c_recv.at[n], me_s, partner)

    c_copies = [c_copy(0, low, part_l), c_copy(1, upp, part_u), c_copy(2, piv, part_p)]
    for copy in c_copies:
        copy.start()
    for ch in range(2):
        f_local(ch).start()

        def start_f(o, carry):
            f_copy(ch, o).start()
            return carry

        lax.fori_loop(1, S, start_f, 0)

    def by_row(ref, first, dst, at):
        def step(g, carry):
            for j in range(F):
                tmp[pl.ds(j * 32, 32), :] = ref[g * F + j, pl.ds(first, 32), :].astype(jnp.float32)
            for j in range(F):
                for y in range(4):
                    dst[at * 4 + y, g // F, j, lax.rem(g, F)] = tmp[pl.ds(j * 32 + y, 8, stride=4), :]
            return carry

        lax.fori_loop(0, 2 * F, step, 0)

    mine = pl.multiple_of(core * 32, 32)
    by_row(low, mine, lf, core)
    by_row(upp, mine, uf, core)
    by_row(piv, mine, pf, core)
    c_copies[0].wait()
    by_row(part_l, 0, lf, other)
    c_copies[1].wait()
    by_row(part_u, 0, uf, other)
    c_copies[2].wait()
    by_row(part_p, 0, pf, other)

    def forward_column(n, carry):
        v = (-lf[0, 0, n], -lf[0, 1, n])
        pre[0, 0, n] = v[0]
        pre[0, 1, n] = v[1]

        def step(y, v):
            w = apply(lf, y, [v])[0]
            w = (-w[0], -w[1])
            pre[y, 0, n] = w[0]
            pre[y, 1, n] = w[1]
            return w

        v = lax.fori_loop(1, ROWS, step, v)
        tm[0, 0, n] = v[0]
        tm[0, 1, n] = v[1]
        return carry

    lax.fori_loop(0, F, forward_column, 0)

    def backward_column(n, carry):
        last = ROWS - 1
        v = (-uf[last, 0, n], -uf[last, 1, n])
        b = (pre[last, 0, n], pre[last, 1, n])

        def step(t, state):
            y = last - 1 - t
            v, b = state
            x, z = apply(uf, y, [v, b])
            return ((-x[0], -x[1]), (pre[y, 0, n] - z[0], pre[y, 1, n] - z[1]))

        v, b = lax.fori_loop(0, last, step, (v, b))
        tm[1, 0, n] = v[0]
        tm[1, 1, n] = v[1]
        tm[2, 0, n] = b[0]
        tm[2, 1, n] = b[1]
        return carry

    lax.fori_loop(0, F, backward_column, 0)

    def halves(p, q):
        axis = p.ndim - 1
        left = lax.broadcasted_iota(jnp.int32, p.shape, axis) < 64
        return (
            jnp.where(left, p, pltpu.roll(q, 64, axis)),
            jnp.where(left, pltpu.roll(p, 64, axis), q),
        )

    def pack_t(g, carry):
        d0, d1 = halves(tm[g // F, 0, lax.rem(g, F)], tm[g // F, 1, lax.rem(g, F)])
        for i in range(F):
            send_t[pl.ds(g * F + i, 8, stride=TR), :] = d0[i]
            send_t[pl.ds(8 * TR + g * F + i, 8, stride=TR), :] = d1[i]
        return carry

    lax.fori_loop(0, 3 * F, pack_t, 0)

    def t_block(k):
        return pl.ds(pl.multiple_of(k * TR, 8), TR)

    def t_copy(o):
        to = wall_peer(o)
        return remote(send_t.at[t_block(to)], recv_t.at[t_block(chip)], t_send.at[to], t_recv.at[chip], me_s, to * 2 + core)

    def t_wait(o):
        frm = wall_peer(o)
        return remote(send_t.at[t_block(frm)], recv_t.at[t_block(frm)], t_send.at[frm], t_recv.at[frm], me_s, frm * 2 + core)

    t_local = pltpu.make_async_copy(send_t.at[t_block(chip)], recv_t.at[t_block(chip)], loc.at[1, 0])
    t_local.start()

    def start_t(o, carry):
        t_copy(o).start()
        return carry

    lax.fori_loop(1, K, start_t, 0)

    def build(f, carry):
        fr = factor[f, 0:1, :]
        fi = factor[f, 1:2, :]
        cosine = table[0]
        sine = table[1]
        gr = cosine * fr - sine * fi
        gi = cosine * fi + sine * fr
        dot = functools.partial(jnp.dot, precision=HI, preferred_element_type=jnp.float32)
        kr = (dot(gr, cosine) + dot(gi, sine)) * (1.0 / 128.0)
        ki = (dot(gi, cosine) - dot(gr, sine)) * (1.0 / 128.0)
        for rows, cols, block in ((0, 0, kr), (0, 128, -ki), (128, 0, ki), (128, 128, kr)):
            top = block.astype(jnp.bfloat16)
            a_hi[f, rows:rows + 128, cols:cols + 128] = top
            a_lo[f, rows:rows + 128, cols:cols + 128] = (block - top.astype(jnp.float32)).astype(jnp.bfloat16)
        return carry

    lax.fori_loop(0, F, build, 0)

    def r_copy(ch, o, d):
        to = span_peer(o)
        c = core if d == 0 else other
        slot = core * S + me_s
        return remote(
            send_r.at[ch, to, c], driv.at[ch, slot], r_send.at[ch, c * S + to], r_recv.at[ch, slot], to, chip * 2 + c
        )

    def r_wait(ch, o, d):
        frm = span_peer(o)
        c = core if d == 0 else other
        slot = c * S + frm
        return remote(
            send_r.at[ch, frm, c], driv.at[ch, slot], r_send.at[ch, slot], r_recv.at[ch, slot], frm, chip * 2 + c
        )

    def r_local(ch):
        return pltpu.make_async_copy(send_r.at[ch, me_s, core], driv.at[ch, core * S + me_s], loc.at[2, ch])

    def filtered(ch, carry):
        f_local(ch).wait()

        def wait_f(o, carry):
            f_wait(ch, o).wait_recv()
            return carry

        lax.fori_loop(1, S, wait_f, 0)

        def field(f, carry):
            rhs = jnp.concatenate(
                [recv_f[ch, :, f, 0].reshape(128, 128), recv_f[ch, :, f, 1].reshape(128, 128)], axis=0
            )
            res = jnp.dot(a_hi[f], rhs, preferred_element_type=jnp.float32) + jnp.dot(
                a_lo[f], rhs, preferred_element_type=jnp.float32
            )
            send_r[ch, :, :, f, 0] = res[:128].reshape(S, 2, 8, 128)
            send_r[ch, :, :, f, 1] = res[128:].reshape(S, 2, 8, 128)
            return carry

        lax.fori_loop(0, F, field, 0)
        r_local(ch).start()
        r_copy(ch, 0, 1).start()

        def start_r(o, carry):
            r_copy(ch, o, 0).start()
            r_copy(ch, o, 1).start()
            return carry

        lax.fori_loop(1, S, start_r, 0)
        return carry

    lax.fori_loop(0, 2, filtered, 0)

    def a_block(ch, k):
        return pl.ds(pl.multiple_of((ch * K + k) * AR, 8), AR)

    def a_copy(ch, o):
        to = wall_peer(o)
        return remote(
            send_a.at[a_block(ch, to)], recv_a.at[a_block(ch, chip)], a_send.at[ch, to], a_recv.at[ch, chip], me_s, to * 2 + core
        )

    def a_wait(ch, o):
        frm = wall_peer(o)
        return remote(
            send_a.at[a_block(ch, frm)], recv_a.at[a_block(ch, frm)], a_send.at[ch, frm], a_recv.at[ch, frm], me_s, frm * 2 + core
        )

    def a_local(ch):
        return pltpu.make_async_copy(send_a.at[a_block(ch, chip)], recv_a.at[a_block(ch, chip)], loc.at[3, ch])

    zero = jnp.zeros((F, 8, 128), jnp.float32)

    def put(ref, y, state):
        for n in range(2):
            ref[y, n, 0] = state[n][0]
            ref[y, n, 1] = state[n][1]

    def get(ref, y):
        return [(ref[y, n, 0], ref[y, n, 1]) for n in range(2)]

    def local_solve(ch, carry):
        r_local(ch).wait()
        r_wait(ch, 0, 1).wait_recv()

        def wait_r(o, carry):
            r_wait(ch, o, 0).wait_recv()
            r_wait(ch, o, 1).wait_recv()
            return carry

        lax.fori_loop(1, S, wait_r, 0)

        def forward(y, state):
            base = (y // 4) * S + lax.rem(y, 4)
            drive = [(driv[ch, base + 4 * n, :, 0], driv[ch, base + 4 * n, :, 1]) for n in range(2)]
            source = apply(pf, y, drive)
            put(src.at[ch], y, source)
            state = sub(source, apply(lf, y, state))
            put(sw, y, state)
            return state

        a = lax.fori_loop(0, ROWS, forward, [(zero, zero), (zero, zero)])

        def backward(t, state):
            y = ROWS - 2 - t
            return sub(get(sw, y), apply(uf, y, state))

        c = lax.fori_loop(0, ROWS - 1, backward, a)
        base = ch * (K * AR)
        for g, (p, q) in enumerate(((a[0][0], a[1][0]), (a[0][1], a[1][1]), (c[0][0], c[1][0]), (c[0][1], c[1][1]))):
            d0, d1 = halves(p, q)
            for i in range(F):
                send_a[pl.ds(base + g * F + i, 8, stride=AR), :] = d0[i]
                send_a[pl.ds(base + 8 * AR + g * F + i, 8, stride=AR), :] = d1[i]
        a_local(ch).start()

        def start_a(o, carry):
            a_copy(ch, o).start()
            return carry

        lax.fori_loop(1, K, start_a, 0)
        return carry

    lax.fori_loop(0, 2, local_solve, 0)

    t_local.wait()

    def wait_t(o, carry):
        t_wait(o).wait_recv()
        return carry

    lax.fori_loop(1, K, wait_t, 0)

    def expand(k, carry):
        for g in range(3 * F):
            rows = recv_t[pl.ds(k * TR + g * F, F), :]
            left = lax.broadcasted_iota(jnp.int32, rows.shape, 1) < 64
            turned = pltpu.roll(rows, 64, 1)
            te[k, g // F, 0, g % F, 0:F, :] = jnp.where(left, rows, turned)
            te[k, g // F, 1, g % F, 0:F, :] = jnp.where(left, turned, rows)
        return carry

    lax.fori_loop(0, K, expand, 0)

    def small(k, m, state, start):
        re, im = start
        for j in range(F):
            tr = te[k, m, 0, j, 0:F, :]
            ti = te[k, m, 1, j, 0:F, :]
            xr = state[0][j:j + 1]
            xi = state[1][j:j + 1]
            re = re + (tr * xr - ti * xi)
            im = im + (tr * xi + ti * xr)
        return re, im

    def s_copy(ch, o):
        to = wall_peer(o)
        return remote(
            send_s.at[a_block(ch, to)], recv_s.at[a_block(ch, chip)], s_send.at[ch, to], s_recv.at[ch, chip], me_s, to * 2 + core
        )

    def s_wait(ch, o):
        frm = wall_peer(o)
        return remote(
            send_s.at[a_block(ch, frm)], recv_s.at[a_block(ch, frm)], s_send.at[ch, frm], s_recv.at[ch, frm], me_s, frm * 2 + core
        )

    def s_local(ch):
        return pltpu.make_async_copy(send_s.at[a_block(ch, chip)], recv_s.at[a_block(ch, chip)], loc.at[4, ch])

    flat = jnp.zeros((F, 128), jnp.float32)

    def owner_scan(ch, carry):
        a_local(ch).wait()

        def wait_a(o, carry):
            a_wait(ch, o).wait_recv()
            return carry

        lax.fori_loop(1, K, wait_a, 0)

        def forward(k, state):
            base = (ch * K + k) * AR
            send_s[pl.ds(base, F), :] = state[0]
            send_s[pl.ds(base + F, F), :] = state[1]
            a = (recv_a[pl.ds(base, F), :], recv_a[pl.ds(base + F, F), :])
            c = (recv_a[pl.ds(base + 2 * F, F), :], recv_a[pl.ds(base + 3 * F, F), :])
            q = small(k, 2, state, c)
            qb[k, 0, 0:F, :] = q[0]
            qb[k, 1, 0:F, :] = q[1]
            return small(k, 0, state, a)

        lax.fori_loop(0, K, forward, (flat, flat))

        def backward(t, state):
            k = K - 1 - t
            base = (ch * K + k) * AR
            send_s[pl.ds(base + 2 * F, F), :] = state[0]
            send_s[pl.ds(base + 3 * F, F), :] = state[1]
            return small(k, 1, state, (qb[k, 0, 0:F, :], qb[k, 1, 0:F, :]))

        lax.fori_loop(0, K, backward, (flat, flat))
        s_local(ch).start()

        def start_s(o, carry):
            s_copy(ch, o).start()
            return carry

        lax.fori_loop(1, K, start_s, 0)
        return carry

    lax.fori_loop(0, 2, owner_scan, 0)

    def o_copy(ch):
        return remote(
            resp.at[other, ch], out.at[:, pl.ds(2 * ch, 2), pl.ds(core * 32, 32), :],
            o_send.at[ch], o_recv.at[ch], me_s, partner,
        )

    def o_wait(ch):
        return remote(
            resp.at[other, ch], out.at[:, pl.ds(2 * ch, 2), pl.ds(other * 32, 32), :],
            o_send.at[ch], o_recv.at[ch], me_s, partner,
        )

    def o_local(ch):
        return pltpu.make_async_copy(
            resp.at[core, ch], out.at[:, pl.ds(2 * ch, 2), pl.ds(core * 32, 32), :], loc.at[5, ch]
        )

    def final(ch, carry):
        s_local(ch).wait()

        def wait_s(o, carry):
            s_wait(ch, o).wait_recv()
            return carry

        lax.fori_loop(1, K, wait_s, 0)
        base = ch * (K * AR)

        def entering(g):
            e0 = jnp.stack([recv_s[pl.ds(base + g * F + i, 8, stride=AR), :] for i in range(F)])
            e1 = jnp.stack([recv_s[pl.ds(base + 8 * AR + g * F + i, 8, stride=AR), :] for i in range(F)])
            return halves(e0, e1)

        def pair(g):
            re = entering(g)
            im = entering(g + 1)
            return [(re[0], im[0]), (re[1], im[1])]

        def forward(y, state):
            state = sub(get(src.at[ch], y), apply(lf, y, state))
            put(sw, y, state)
            return state

        lax.fori_loop(0, ROWS, forward, pair(0))

        def backward(t, state):
            y = ROWS - 1 - t
            state = sub(get(sw, y), apply(uf, y, state))
            for n in range(2):
                for ri in range(2):
                    for i in range(F):
                        resp.at[y // 4, ch, ri * F + i, n][pl.ds(lax.rem(y, 4), 8, stride=4), :] = state[n][ri][i]
            return state

        lax.fori_loop(0, ROWS, backward, pair(2))
        o_local(ch).start()
        o_copy(ch).start()
        return carry

    lax.fori_loop(0, 2, final, 0)

    for ch in range(2):
        o_local(ch).wait()
        o_wait(ch).wait_recv()
        o_copy(ch).wait_send()
        r_copy(ch, 0, 1).wait_send()

        def end_span(o, carry):
            f_copy(ch, o).wait_send()
            r_copy(ch, o, 0).wait_send()
            r_copy(ch, o, 1).wait_send()
            return carry

        def end_wall(o, carry):
            a_copy(ch, o).wait_send()
            s_copy(ch, o).wait_send()
            return carry

        lax.fori_loop(1, S, end_span, 0)
        lax.fori_loop(1, K, end_wall, 0)

    def end_t(o, carry):
        t_copy(o).wait_send()
        return carry

    lax.fori_loop(1, K, end_t, 0)


def tables():
    n = np.arange(128)
    angle = (n[:, None] * n[None, :] % 128) * (2.0 * math.pi / 128)
    return np.stack([np.cos(angle), np.sin(angle)]).astype(np.float32)


def local(forcing, span_factor, pivot_inverse, step_lower, step_upper):
    f32, bf16 = jnp.float32, jnp.bfloat16
    dma = pltpu.SemaphoreType.DMA
    vm = pltpu.VMEM
    flat = [x.reshape(50, 64, 128) for x in (pivot_inverse, step_lower, step_upper)]
    coef = vm((ROWS, 2, F, F, 8, 128), f32)
    rows = vm((ROWS, 2, 2, F, 8, 128), f32)
    scratch = [
        vm((256, 128), f32),
        vm((2, S, F, 2, 16, 128), bf16),
        vm((2, S, F, 2, 16, 128), bf16),
        vm((50, 32, 128), bf16), vm((50, 32, 128), bf16), vm((50, 32, 128), bf16),
        coef, coef, coef, coef,
        vm((3, 2, F, F, 8, 128), f32),
        vm((F, 256, 256), bf16), vm((F, 256, 256), bf16),
        vm((2, S, 2, F, 2, 8, 128), f32),
        vm((2, 2 * S, F, 2, 8, 128), f32),
        vm((K * TR, 128), f32), vm((K * TR, 128), f32),
        vm((K, 3, 2, F, 8, 128), f32),
        vm((2 * K * AR, 128), f32), vm((2 * K * AR, 128), f32),
        vm((2 * K * AR, 128), f32), vm((2 * K * AR, 128), f32),
        vm((2, ROWS, 2, 2, F, 8, 128), f32),
        rows,
        vm((K, 2, 8, 128), f32),
        vm((2, 2, 2 * F, 2, 32, 128), f32),
        dma((3,)), dma((3,)),
        dma((2, S)), dma((2, S)),
        dma((2, 2 * S)), dma((2, 2 * S)),
        dma((K,)), dma((K,)),
        dma((2, K)), dma((2, K)),
        dma((2, K)), dma((2, K)),
        dma((2,)), dma((2,)),
        dma((6, 2)),
    ]
    out = pl.pallas_call(
        kernel,
        out_shape=jax.ShapeDtypeStruct((2 * F, 4, 64, 128), f32),
        in_specs=[pl.BlockSpec(memory_space=pltpu.VMEM)] * 6,
        out_specs=pl.BlockSpec(memory_space=pltpu.VMEM),
        scratch_shapes=scratch,
        compiler_params=pltpu.CompilerParams(
            collective_id=0, has_side_effects=True, vmem_limit_bytes=56 << 20
        ),
    )(
        forcing.reshape(2 * F, 4, 64, 128),
        jnp.swapaxes(span_factor, 0, 1),
        jnp.asarray(tables()),
        *flat,
    )
    return out.reshape(2, F, 4, 16, 4, 128)


def solution(mesh):
    placed = P(None, None, None, "span", "wall", None)
    return jax.shard_map(
        local,
        mesh=mesh,
        in_specs=(placed, P(), placed, placed, placed),
        out_specs=placed,
        check_vma=False,
    )
```

```python
import functools
import math

import jax
import jax.numpy as jnp
import numpy as np
from jax import lax
from jax.experimental import pallas as pl
from jax.experimental.pallas import tpu as pltpu
from jax.sharding import PartitionSpec as P

MESH = pl.DeviceIdType.MESH
F = 5
S = 8
K = 16
ROWS = 8
TR = 80
AR = 24
HI = lax.Precision.HIGHEST
LEVELS = 29900.0
SHIFT = 117.0


def encode(x, scale):
    y = x * (LEVELS / scale)
    n = jnp.floor(jnp.abs(y) + 0.5)
    e = jnp.floor(n * (1.0 / 128.0))
    v = (1.0 + (n - 128.0 * e) * (1.0 / 128.0)) * jnp.exp2(e - SHIFT)
    return jnp.where(y < 0.0, -v, v)


def decode(v, scale):
    a = jnp.abs(v)
    e = jnp.floor(jnp.log2(a) + 0.002)
    n = 128.0 * (e + (SHIFT - 1.0)) + 128.0 * (a * jnp.exp2(-e))
    return jnp.where(v < 0.0, -n, n) * (scale * (1.0 / LEVELS))


def apply(coef, y, vectors):
    out = [None] * len(vectors)
    for j in range(F):
        cr = coef[y, 0, j]
        ci = coef[y, 1, j]
        for n, (vr, vi) in enumerate(vectors):
            xr = vr[j][None]
            xi = vi[j][None]
            re = cr * xr - ci * xi
            im = cr * xi + ci * xr
            out[n] = (re, im) if out[n] is None else (out[n][0] + re, out[n][1] + im)
    return out


def sub(a, b):
    return [(x[0] - y[0], x[1] - y[1]) for x, y in zip(a, b)]


def kernel(
    forcing_in, factor_in, table_in, piv_in, low_in, upp_in, out,
    forcing, factor, table, piv, low, upp, tmp, scales, send_f, recv_f, part_p, part_l, part_u, pf, lf, uf, pre, tm, a_hi, a_lo,
    send_r, driv, send_t, recv_t, te, send_a, recv_a, send_s, recv_s, src, sw, qb, resp,
    c_send, c_recv, f_send, f_recv, r_send, r_recv, t_send, t_recv, a_send, a_recv, s_send, s_recv,
    o_send, o_recv, loc, load,
):
    me_s = lax.axis_index("span")
    me_w = lax.axis_index("wall")
    core = lax.rem(me_w, 2)
    chip = me_w // 2
    other = 1 - core
    partner = chip * 2 + other

    def span_peer(o):
        return lax.rem(me_s + o, S)

    def wall_peer(o):
        return lax.rem(chip + o, K)

    loads = [
        pltpu.make_async_copy(a, b, load.at[n])
        for n, (a, b) in enumerate(
            (
                (forcing_in, forcing), (low_in, low), (upp_in, upp), (piv_in, piv),
                (factor_in, factor), (table_in, table),
            )
        )
    ]
    for copy in loads:
        copy.start()

    barrier = pltpu.get_barrier_semaphore()

    def greet(s, w):
        pl.semaphore_signal(barrier, inc=1, device_id=(s, w), device_id_type=MESH)

    def greet_span(o, carry):
        greet(span_peer(o), me_w)
        greet(span_peer(o), partner)
        return carry

    def greet_wall(o, carry):
        greet(me_s, wall_peer(o) * 2 + core)
        return carry

    lax.fori_loop(1, S, greet_span, 0)
    lax.fori_loop(1, K, greet_wall, 0)
    greet(me_s, partner)

    def regroup(g, carry):
        for col in range(4):
            tmp[pl.ds(col * 64, 64), :] = forcing[g, col].astype(jnp.float32)
        for col in range(4):
            for y in range(4):
                piece = tmp[pl.ds(col * 64 + y, 16, stride=4), :].astype(jnp.bfloat16)
                send_f[col // 2, (col % 2) * 4 + y, lax.rem(g, F), g // F] = piece
        return carry

    loads[0].wait()
    lax.fori_loop(0, 2 * F, regroup, 0)
    for copy in loads[1:]:
        copy.wait()

    pl.semaphore_wait(barrier, 2 * S - 1 + K - 1)

    def remote(src_ref, dst_ref, ss, rs, s, w):
        return pltpu.make_async_remote_copy(
            src_ref=src_ref, dst_ref=dst_ref, send_sem=ss, recv_sem=rs,
            device_id=(s, w), device_id_type=MESH,
        )

    def f_copy(ch, o):
        to = span_peer(o)
        return remote(send_f.at[ch, to], recv_f.at[ch, me_s], f_send.at[ch, to], f_recv.at[ch, me_s], to, me_w)

    def f_wait(ch, o):
        frm = span_peer(o)
        return remote(send_f.at[ch, frm], recv_f.at[ch, frm], f_send.at[ch, frm], f_recv.at[ch, frm], frm, me_w)

    def f_local(ch):
        return pltpu.make_async_copy(send_f.at[ch, me_s], recv_f.at[ch, me_s], loc.at[0, ch])

    def c_copy(n, ref, part):
        return remote(ref.at[:, pl.ds(other * 32, 32), :], part, c_send.at[n], c_recv.at[n], me_s, partner)

    c_copies = [c_copy(0, low, part_l), c_copy(1, upp, part_u), c_copy(2, piv, part_p)]
    for copy in c_copies:
        copy.start()
    for ch in range(2):
        f_local(ch).start()

        def start_f(o, carry):
            f_copy(ch, o).start()
            return carry

        lax.fori_loop(1, S, start_f, 0)

    def by_row(ref, first, dst, at):
        def step(g, carry):
            for j in range(F):
                tmp[pl.ds(j * 32, 32), :] = ref[g * F + j, pl.ds(first, 32), :].astype(jnp.float32)
            for j in range(F):
                for y in range(4):
                    dst[at * 4 + y, g // F, j, lax.rem(g, F)] = tmp[pl.ds(j * 32 + y, 8, stride=4), :]
            return carry

        lax.fori_loop(0, 2 * F, step, 0)

    mine = pl.multiple_of(core * 32, 32)
    by_row(low, mine, lf, core)
    by_row(upp, mine, uf, core)
    by_row(piv, mine, pf, core)
    def build(f, carry):
        fr = factor[f, 0:1, :]
        fi = factor[f, 1:2, :]
        cosine = table[0]
        sine = table[1]
        gr = cosine * fr - sine * fi
        gi = cosine * fi + sine * fr
        dot = functools.partial(jnp.dot, precision=HI, preferred_element_type=jnp.float32)
        kr = (dot(gr, cosine) + dot(gi, sine)) * (1.0 / 128.0)
        ki = (dot(gi, cosine) - dot(gr, sine)) * (1.0 / 128.0)
        for rows, cols, block in ((0, 0, kr), (0, 128, -ki), (128, 0, ki), (128, 128, kr)):
            top = block.astype(jnp.bfloat16)
            a_hi[f, rows:rows + 128, cols:cols + 128] = top
            a_lo[f, rows:rows + 128, cols:cols + 128] = (block - top.astype(jnp.float32)).astype(jnp.bfloat16)
        return carry

    lax.fori_loop(0, F, build, 0)

    c_copies[0].wait()
    by_row(part_l, 0, lf, other)
    c_copies[1].wait()
    by_row(part_u, 0, uf, other)
    c_copies[2].wait()
    by_row(part_p, 0, pf, other)

    def forward_column(n, carry):
        v = (-lf[0, 0, n], -lf[0, 1, n])
        pre[0, 0, n] = v[0]
        pre[0, 1, n] = v[1]

        def step(y, v):
            w = apply(lf, y, [v])[0]
            w = (-w[0], -w[1])
            pre[y, 0, n] = w[0]
            pre[y, 1, n] = w[1]
            return w

        v = lax.fori_loop(1, ROWS, step, v)
        tm[0, 0, n] = v[0]
        tm[0, 1, n] = v[1]
        return carry

    lax.fori_loop(0, F, forward_column, 0)

    def backward_column(n, carry):
        last = ROWS - 1
        v = (-uf[last, 0, n], -uf[last, 1, n])
        b = (pre[last, 0, n], pre[last, 1, n])

        def step(t, state):
            y = last - 1 - t
            v, b = state
            x, z = apply(uf, y, [v, b])
            return ((-x[0], -x[1]), (pre[y, 0, n] - z[0], pre[y, 1, n] - z[1]))

        v, b = lax.fori_loop(0, last, step, (v, b))
        tm[1, 0, n] = v[0]
        tm[1, 1, n] = v[1]
        tm[2, 0, n] = b[0]
        tm[2, 1, n] = b[1]
        return carry

    lax.fori_loop(0, F, backward_column, 0)

    def halves(p, q):
        axis = p.ndim - 1
        left = lax.broadcasted_iota(jnp.int32, p.shape, axis) < 64
        return (
            jnp.where(left, p, pltpu.roll(q, 64, axis)),
            jnp.where(left, pltpu.roll(p, 64, axis), q),
        )

    def pack_t(g, carry):
        d0, d1 = halves(tm[g // F, 0, lax.rem(g, F)], tm[g // F, 1, lax.rem(g, F)])
        for i in range(F):
            send_t[pl.ds(g * F + i, 8, stride=TR), :] = d0[i]
            send_t[pl.ds(8 * TR + g * F + i, 8, stride=TR), :] = d1[i]
        return carry

    lax.fori_loop(0, 3 * F, pack_t, 0)

    def t_block(k):
        return pl.ds(pl.multiple_of(k * TR, 8), TR)

    def t_copy(o):
        to = wall_peer(o)
        return remote(send_t.at[t_block(to)], recv_t.at[t_block(chip)], t_send.at[to], t_recv.at[chip], me_s, to * 2 + core)

    def t_wait(o):
        frm = wall_peer(o)
        return remote(send_t.at[t_block(frm)], recv_t.at[t_block(frm)], t_send.at[frm], t_recv.at[frm], me_s, frm * 2 + core)

    t_local = pltpu.make_async_copy(send_t.at[t_block(chip)], recv_t.at[t_block(chip)], loc.at[1, 0])
    t_local.start()

    def start_t(o, carry):
        t_copy(o).start()
        return carry

    lax.fori_loop(1, K, start_t, 0)

    def r_copy(ch, o, d):
        to = span_peer(o)
        c = core if d == 0 else other
        slot = core * S + me_s
        return remote(
            send_r.at[ch, to, c], driv.at[ch, slot], r_send.at[ch, c * S + to], r_recv.at[ch, slot], to, chip * 2 + c
        )

    def r_wait(ch, o, d):
        frm = span_peer(o)
        c = core if d == 0 else other
        slot = c * S + frm
        return remote(
            send_r.at[ch, frm, c], driv.at[ch, slot], r_send.at[ch, slot], r_recv.at[ch, slot], frm, chip * 2 + c
        )

    def r_local(ch):
        return pltpu.make_async_copy(send_r.at[ch, me_s, core], driv.at[ch, core * S + me_s], loc.at[2, ch])

    def filtered(ch, carry):
        f_local(ch).wait()

        def wait_f(o, carry):
            f_wait(ch, o).wait_recv()
            return carry

        lax.fori_loop(1, S, wait_f, 0)

        def field(f, carry):
            rhs = jnp.concatenate(
                [recv_f[ch, :, f, 0].reshape(128, 128), recv_f[ch, :, f, 1].reshape(128, 128)], axis=0
            )
            res = jnp.dot(a_hi[f], rhs, preferred_element_type=jnp.float32) + jnp.dot(
                a_lo[f], rhs, preferred_element_type=jnp.float32
            )
            re = res[:128].reshape(S, 2, 8, 128)
            im = res[128:].reshape(S, 2, 8, 128)
            top = jnp.max(jnp.maximum(jnp.abs(re), jnp.abs(im)), axis=2, keepdims=True)
            scale = jnp.maximum(top * 1.01, 1e-30).astype(jnp.bfloat16).astype(jnp.float32)
            scales[:, :, pl.ds(f, 1), :] = scale
            codes = jnp.concatenate([encode(re, scale), encode(im, scale)], axis=2)
            send_r[ch, :, :, f] = codes.astype(jnp.bfloat16)
            return carry

        lax.fori_loop(0, F, field, 0)
        send_r[ch, :, :, F] = jnp.concatenate([scales[...], scales[...]], axis=2).astype(jnp.bfloat16)
        r_local(ch).start()
        r_copy(ch, 0, 1).start()

        def start_r(o, carry):
            r_copy(ch, o, 0).start()
            r_copy(ch, o, 1).start()
            return carry

        lax.fori_loop(1, S, start_r, 0)
        return carry

    lax.fori_loop(0, 2, filtered, 0)

    def a_block(ch, k):
        return pl.ds(pl.multiple_of((ch * K + k) * AR, 8), AR)

    def a_copy(ch, o):
        to = wall_peer(o)
        return remote(
            send_a.at[a_block(ch, to)], recv_a.at[a_block(ch, chip)], a_send.at[ch, to], a_recv.at[ch, chip], me_s, to * 2 + core
        )

    def a_wait(ch, o):
        frm = wall_peer(o)
        return remote(
            send_a.at[a_block(ch, frm)], recv_a.at[a_block(ch, frm)], a_send.at[ch, frm], a_recv.at[ch, frm], me_s, frm * 2 + core
        )

    def a_local(ch):
        return pltpu.make_async_copy(send_a.at[a_block(ch, chip)], recv_a.at[a_block(ch, chip)], loc.at[3, ch])

    zero = jnp.zeros((F, 8, 128), jnp.float32)

    def put(ref, y, state):
        for n in range(2):
            ref[y, n, 0] = state[n][0]
            ref[y, n, 1] = state[n][1]

    def get(ref, y):
        return [(ref[y, n, 0], ref[y, n, 1]) for n in range(2)]

    def local_solve(ch, carry):
        r_local(ch).wait()
        r_wait(ch, 0, 1).wait_recv()

        def wait_r(o, carry):
            r_wait(ch, o, 0).wait_recv()
            r_wait(ch, o, 1).wait_recv()
            return carry

        lax.fori_loop(1, S, wait_r, 0)

        def forward(y, state):
            base = (y // 4) * S + lax.rem(y, 4)
            drive = []
            for n in range(2):
                scale = driv[ch, base + 4 * n, F].astype(jnp.float32)
                parts = [
                    decode(driv[ch, base + 4 * n, f].astype(jnp.float32), scale[f:f + 1]) for f in range(F)
                ]
                drive.append((jnp.stack([x[:8] for x in parts]), jnp.stack([x[8:] for x in parts])))
            source = apply(pf, y, drive)
            put(src.at[ch], y, source)
            state = sub(source, apply(lf, y, state))
            put(sw, y, state)
            return state

        a = lax.fori_loop(0, ROWS, forward, [(zero, zero), (zero, zero)])

        def backward(t, state):
            y = ROWS - 2 - t
            return sub(get(sw, y), apply(uf, y, state))

        c = lax.fori_loop(0, ROWS - 1, backward, a)
        base = ch * (K * AR)
        for g, (p, q) in enumerate(((a[0][0], a[1][0]), (a[0][1], a[1][1]), (c[0][0], c[1][0]), (c[0][1], c[1][1]))):
            d0, d1 = halves(p, q)
            for i in range(F):
                send_a[pl.ds(base + g * F + i, 8, stride=AR), :] = d0[i]
                send_a[pl.ds(base + 8 * AR + g * F + i, 8, stride=AR), :] = d1[i]
        a_local(ch).start()

        def start_a(o, carry):
            a_copy(ch, o).start()
            return carry

        lax.fori_loop(1, K, start_a, 0)
        return carry

    lax.fori_loop(0, 2, local_solve, 0)

    t_local.wait()

    def wait_t(o, carry):
        t_wait(o).wait_recv()
        return carry

    lax.fori_loop(1, K, wait_t, 0)

    def expand(k, carry):
        for g in range(3 * F):
            rows = recv_t[pl.ds(k * TR + g * F, F), :]
            left = lax.broadcasted_iota(jnp.int32, rows.shape, 1) < 64
            turned = pltpu.roll(rows, 64, 1)
            te[k, g // F, 0, g % F, 0:F, :] = jnp.where(left, rows, turned)
            te[k, g // F, 1, g % F, 0:F, :] = jnp.where(left, turned, rows)
        return carry

    lax.fori_loop(0, K, expand, 0)

    def small(k, m, state, start):
        re, im = start
        for j in range(F):
            tr = te[k, m, 0, j, 0:F, :]
            ti = te[k, m, 1, j, 0:F, :]
            xr = state[0][j:j + 1]
            xi = state[1][j:j + 1]
            re = re + (tr * xr - ti * xi)
            im = im + (tr * xi + ti * xr)
        return re, im

    def s_copy(ch, o):
        to = wall_peer(o)
        return remote(
            send_s.at[a_block(ch, to)], recv_s.at[a_block(ch, chip)], s_send.at[ch, to], s_recv.at[ch, chip], me_s, to * 2 + core
        )

    def s_wait(ch, o):
        frm = wall_peer(o)
        return remote(
            send_s.at[a_block(ch, frm)], recv_s.at[a_block(ch, frm)], s_send.at[ch, frm], s_recv.at[ch, frm], me_s, frm * 2 + core
        )

    def s_local(ch):
        return pltpu.make_async_copy(send_s.at[a_block(ch, chip)], recv_s.at[a_block(ch, chip)], loc.at[4, ch])

    flat = jnp.zeros((F, 128), jnp.float32)

    def owner_scan(ch, carry):
        a_local(ch).wait()

        def wait_a(o, carry):
            a_wait(ch, o).wait_recv()
            return carry

        lax.fori_loop(1, K, wait_a, 0)

        def forward(k, state):
            base = (ch * K + k) * AR
            send_s[pl.ds(base, F), :] = state[0]
            send_s[pl.ds(base + F, F), :] = state[1]
            a = (recv_a[pl.ds(base, F), :], recv_a[pl.ds(base + F, F), :])
            c = (recv_a[pl.ds(base + 2 * F, F), :], recv_a[pl.ds(base + 3 * F, F), :])
            q = small(k, 2, state, c)
            qb[k, 0, 0:F, :] = q[0]
            qb[k, 1, 0:F, :] = q[1]
            return small(k, 0, state, a)

        lax.fori_loop(0, K, forward, (flat, flat))

        def backward(t, state):
            k = K - 1 - t
            base = (ch * K + k) * AR
            send_s[pl.ds(base + 2 * F, F), :] = state[0]
            send_s[pl.ds(base + 3 * F, F), :] = state[1]
            return small(k, 1, state, (qb[k, 0, 0:F, :], qb[k, 1, 0:F, :]))

        lax.fori_loop(0, K, backward, (flat, flat))
        s_local(ch).start()

        def start_s(o, carry):
            s_copy(ch, o).start()
            return carry

        lax.fori_loop(1, K, start_s, 0)
        return carry

    lax.fori_loop(0, 2, owner_scan, 0)

    def o_copy(ch):
        return remote(
            resp.at[other, ch], out.at[:, pl.ds(2 * ch, 2), pl.ds(core * 32, 32), :],
            o_send.at[ch], o_recv.at[ch], me_s, partner,
        )

    def o_wait(ch):
        return remote(
            resp.at[other, ch], out.at[:, pl.ds(2 * ch, 2), pl.ds(other * 32, 32), :],
            o_send.at[ch], o_recv.at[ch], me_s, partner,
        )

    def o_local(ch):
        return pltpu.make_async_copy(
            resp.at[core, ch], out.at[:, pl.ds(2 * ch, 2), pl.ds(core * 32, 32), :], loc.at[5, ch]
        )

    def final(ch, carry):
        s_local(ch).wait()

        def wait_s(o, carry):
            s_wait(ch, o).wait_recv()
            return carry

        lax.fori_loop(1, K, wait_s, 0)
        base = ch * (K * AR)

        def entering(g):
            e0 = jnp.stack([recv_s[pl.ds(base + g * F + i, 8, stride=AR), :] for i in range(F)])
            e1 = jnp.stack([recv_s[pl.ds(base + 8 * AR + g * F + i, 8, stride=AR), :] for i in range(F)])
            return halves(e0, e1)

        def pair(g):
            re = entering(g)
            im = entering(g + 1)
            return [(re[0], im[0]), (re[1], im[1])]

        def forward(y, state):
            state = sub(get(src.at[ch], y), apply(lf, y, state))
            put(sw, y, state)
            return state

        lax.fori_loop(0, ROWS, forward, pair(0))

        def backward(t, state):
            y = ROWS - 1 - t
            state = sub(get(sw, y), apply(uf, y, state))
            for n in range(2):
                for ri in range(2):
                    for i in range(F):
                        resp.at[y // 4, ch, ri * F + i, n][pl.ds(lax.rem(y, 4), 8, stride=4), :] = state[n][ri][i]
            return state

        lax.fori_loop(0, ROWS, backward, pair(2))
        o_local(ch).start()
        o_copy(ch).start()
        return carry

    lax.fori_loop(0, 2, final, 0)

    for ch in range(2):
        o_local(ch).wait()
        o_wait(ch).wait_recv()
        o_copy(ch).wait_send()
        r_copy(ch, 0, 1).wait_send()

        def end_span(o, carry):
            f_copy(ch, o).wait_send()
            r_copy(ch, o, 0).wait_send()
            r_copy(ch, o, 1).wait_send()
            return carry

        def end_wall(o, carry):
            a_copy(ch, o).wait_send()
            s_copy(ch, o).wait_send()
            return carry

        lax.fori_loop(1, S, end_span, 0)
        lax.fori_loop(1, K, end_wall, 0)

    def end_t(o, carry):
        t_copy(o).wait_send()
        return carry

    lax.fori_loop(1, K, end_t, 0)


def tables():
    n = np.arange(128)
    angle = (n[:, None] * n[None, :] % 128) * (2.0 * math.pi / 128)
    return np.stack([np.cos(angle), np.sin(angle)]).astype(np.float32)


def local(forcing, span_factor, pivot_inverse, step_lower, step_upper):
    f32, bf16 = jnp.float32, jnp.bfloat16
    dma = pltpu.SemaphoreType.DMA
    vm = pltpu.VMEM
    flat = [x.reshape(50, 64, 128) for x in (pivot_inverse, step_lower, step_upper)]
    coef = vm((ROWS, 2, F, F, 8, 128), f32)
    rows = vm((ROWS, 2, 2, F, 8, 128), f32)
    scratch = [
        vm((2 * F, 4, 64, 128), bf16), vm((F, 2, 128), f32), vm((2, 128, 128), f32),
        vm((50, 64, 128), bf16), vm((50, 64, 128), bf16), vm((50, 64, 128), bf16),
        vm((256, 128), f32),
        vm((S, 2, 8, 128), f32),
        vm((2, S, F, 2, 16, 128), bf16),
        vm((2, S, F, 2, 16, 128), bf16),
        vm((50, 32, 128), bf16), vm((50, 32, 128), bf16), vm((50, 32, 128), bf16),
        coef, coef, coef, coef,
        vm((3, 2, F, F, 8, 128), f32),
        vm((F, 256, 256), bf16), vm((F, 256, 256), bf16),
        vm((2, S, 2, F + 1, 16, 128), bf16),
        vm((2, 2 * S, F + 1, 16, 128), bf16),
        vm((K * TR, 128), f32), vm((K * TR, 128), f32),
        vm((K, 3, 2, F, 8, 128), f32),
        vm((2 * K * AR, 128), f32), vm((2 * K * AR, 128), f32),
        vm((2 * K * AR, 128), f32), vm((2 * K * AR, 128), f32),
        vm((2, ROWS, 2, 2, F, 8, 128), f32),
        rows,
        vm((K, 2, 8, 128), f32),
        vm((2, 2, 2 * F, 2, 32, 128), f32),
        dma((3,)), dma((3,)),
        dma((2, S)), dma((2, S)),
        dma((2, 2 * S)), dma((2, 2 * S)),
        dma((K,)), dma((K,)),
        dma((2, K)), dma((2, K)),
        dma((2, K)), dma((2, K)),
        dma((2,)), dma((2,)),
        dma((6, 2)),
        dma((6,)),
    ]
    out = pl.pallas_call(
        kernel,
        out_shape=jax.ShapeDtypeStruct((2 * F, 4, 64, 128), f32),
        in_specs=[pl.BlockSpec(memory_space=pl.ANY)] * 6,
        out_specs=pl.BlockSpec(memory_space=pl.ANY),
        scratch_shapes=scratch,
        compiler_params=pltpu.CompilerParams(
            collective_id=0, has_side_effects=True, vmem_limit_bytes=56 << 20
        ),
    )(
        forcing.reshape(2 * F, 4, 64, 128),
        jnp.swapaxes(span_factor, 0, 1),
        jnp.asarray(tables()),
        *flat,
    )
    return out.reshape(2, F, 4, 16, 4, 128)


def solution(mesh):
    placed = P(None, None, None, "span", "wall", None)
    return jax.shard_map(
        local,
        mesh=mesh,
        in_specs=(placed, P(), placed, placed, placed),
        out_specs=placed,
        check_vma=False,
    )
```

```python
import functools
import math

import jax
import jax.numpy as jnp
import numpy as np
from jax import lax
from jax.experimental import pallas as pl
from jax.experimental.pallas import tpu as pltpu
from jax.sharding import PartitionSpec as P

MESH = pl.DeviceIdType.MESH
F = 5
S = 8
K = 16
ROWS = 8
TR = 96
AR = 24
HI = lax.Precision.HIGHEST
LEVELS = 29900.0
SHIFT = 117.0


def encode(x, scale):
    y = x * (LEVELS / scale)
    n = jnp.floor(jnp.abs(y) + 0.5)
    e = jnp.floor(n * (1.0 / 128.0))
    v = (1.0 + (n - 128.0 * e) * (1.0 / 128.0)) * jnp.exp2(e - SHIFT)
    return jnp.where(y < 0.0, -v, v)


def decode(v, scale):
    a = jnp.abs(v)
    e = jnp.floor(jnp.log2(a) + 0.002)
    n = 128.0 * (e + (SHIFT - 1.0)) + 128.0 * (a * jnp.exp2(-e))
    return jnp.where(v < 0.0, -n, n) * (scale * (1.0 / LEVELS))


def encode_blocks(src, dst, first, count, parts, tiles, used):
    rows = parts * tiles * 8
    x = src[pl.ds(pl.multiple_of(first * rows, 8), count * rows), :].reshape(count * parts, tiles, 8, 128)
    place = lax.broadcasted_iota(jnp.int32, x.shape, 1) * 8 + lax.broadcasted_iota(jnp.int32, x.shape, 2)
    good = place < used
    x = jnp.where(good, x, 0.0)
    top = jnp.max(jnp.max(jnp.abs(x), axis=1, keepdims=True), axis=2, keepdims=True)
    scale = jnp.maximum(top * 1.01, 1e-30).astype(jnp.bfloat16).astype(jnp.float32)
    code = jnp.where(good, encode(x, scale), scale).astype(jnp.bfloat16)
    dst[pl.ds(first, count)] = code.reshape(count, parts * tiles, 8, 128)


def decode_blocks(src, dst, first, count, parts, tiles):
    rows = parts * tiles * 8
    code = src[pl.ds(first, count)].astype(jnp.float32).reshape(count * parts, tiles, 8, 128)
    x = decode(code, code[:, tiles - 1:, 7:, :])
    dst[pl.ds(pl.multiple_of(first * rows, 8), count * rows), :] = x.reshape(count * rows, 128)


def apply(coef, y, vectors):
    out = [None] * len(vectors)
    for j in range(F):
        cr = coef[y, 0, j]
        ci = coef[y, 1, j]
        for n, (vr, vi) in enumerate(vectors):
            xr = vr[j][None]
            xi = vi[j][None]
            re = cr * xr - ci * xi
            im = cr * xi + ci * xr
            out[n] = (re, im) if out[n] is None else (out[n][0] + re, out[n][1] + im)
    return out


def sub(a, b):
    return [(x[0] - y[0], x[1] - y[1]) for x, y in zip(a, b)]


def kernel(
    forcing_in, factor_in, table_in, piv_in, low_in, upp_in, out,
    forcing, factor, table, piv, low, upp, tmp, scales, send_f, recv_f, part_p, part_l, part_u, pf, lf, uf, pre, tm, a_hi, a_lo,
    send_r, driv, send_t, recv_t, te, send_a, recv_a, send_s, recv_s,
    code_t, got_t, code_a, got_a, code_s, got_s, src, sw, qb, resp,
    c_send, c_recv, f_send, f_recv, r_send, r_recv, t_send, t_recv, a_send, a_recv, s_send, s_recv,
    o_send, o_recv, loc, load,
):
    me_s = lax.axis_index("span")
    me_w = lax.axis_index("wall")
    core = lax.rem(me_w, 2)
    chip = me_w // 2
    other = 1 - core
    partner = chip * 2 + other

    def span_peer(o):
        return lax.rem(me_s + o, S)

    def wall_peer(o):
        return lax.rem(chip + o, K)

    loads = [
        pltpu.make_async_copy(a, b, load.at[n])
        for n, (a, b) in enumerate(
            (
                (forcing_in, forcing), (low_in, low), (upp_in, upp), (piv_in, piv),
                (factor_in, factor), (table_in, table),
            )
        )
    ]
    for copy in loads:
        copy.start()

    barrier = pltpu.get_barrier_semaphore()

    def greet(s, w):
        pl.semaphore_signal(barrier, inc=1, device_id=(s, w), device_id_type=MESH)

    def greet_span(o, carry):
        greet(span_peer(o), me_w)
        greet(span_peer(o), partner)
        return carry

    def greet_wall(o, carry):
        greet(me_s, wall_peer(o) * 2 + core)
        return carry

    lax.fori_loop(1, S, greet_span, 0)
    lax.fori_loop(1, K, greet_wall, 0)
    greet(me_s, partner)

    def regroup(g, carry):
        for col in range(4):
            tmp[pl.ds(col * 64, 64), :] = forcing[g, col].astype(jnp.float32)
        for col in range(4):
            for y in range(4):
                piece = tmp[pl.ds(col * 64 + y, 16, stride=4), :].astype(jnp.bfloat16)
                send_f[col // 2, (col % 2) * 4 + y, lax.rem(g, F), g // F] = piece
        return carry

    loads[0].wait()
    lax.fori_loop(0, 2 * F, regroup, 0)
    for copy in loads[1:]:
        copy.wait()

    pl.semaphore_wait(barrier, 2 * S - 1 + K - 1)

    def remote(src_ref, dst_ref, ss, rs, s, w):
        return pltpu.make_async_remote_copy(
            src_ref=src_ref, dst_ref=dst_ref, send_sem=ss, recv_sem=rs,
            device_id=(s, w), device_id_type=MESH,
        )

    def f_copy(ch, o):
        to = span_peer(o)
        return remote(send_f.at[ch, to], recv_f.at[ch, me_s], f_send.at[ch, to], f_recv.at[ch, me_s], to, me_w)

    def f_wait(ch, o):
        frm = span_peer(o)
        return remote(send_f.at[ch, frm], recv_f.at[ch, frm], f_send.at[ch, frm], f_recv.at[ch, frm], frm, me_w)

    def f_local(ch):
        return pltpu.make_async_copy(send_f.at[ch, me_s], recv_f.at[ch, me_s], loc.at[0, ch])

    def c_copy(n, ref, part):
        return remote(ref.at[:, pl.ds(other * 32, 32), :], part, c_send.at[n], c_recv.at[n], me_s, partner)

    c_copies = [c_copy(0, low, part_l), c_copy(1, upp, part_u), c_copy(2, piv, part_p)]
    for copy in c_copies:
        copy.start()

    def forcing_out(ch):
        f_local(ch).start()

        def start_f(o, carry):
            f_copy(ch, o).start()
            return carry

        lax.fori_loop(1, S, start_f, 0)

    forcing_out(0)

    def by_row(ref, first, dst, at):
        def step(g, carry):
            for j in range(F):
                tmp[pl.ds(j * 32, 32), :] = ref[g * F + j, pl.ds(first, 32), :].astype(jnp.float32)
            for j in range(F):
                for y in range(4):
                    dst[at * 4 + y, g // F, j, lax.rem(g, F)] = tmp[pl.ds(j * 32 + y, 8, stride=4), :]
            return carry

        lax.fori_loop(0, 2 * F, step, 0)

    mine = pl.multiple_of(core * 32, 32)
    by_row(low, mine, lf, core)
    by_row(upp, mine, uf, core)
    by_row(piv, mine, pf, core)
    def build(f, carry):
        fr = factor[f, 0:1, :]
        fi = factor[f, 1:2, :]
        cosine = table[0]
        sine = table[1]
        gr = cosine * fr - sine * fi
        gi = cosine * fi + sine * fr
        dot = functools.partial(jnp.dot, precision=HI, preferred_element_type=jnp.float32)
        kr = (dot(gr, cosine) + dot(gi, sine)) * (1.0 / 128.0)
        ki = (dot(gi, cosine) - dot(gr, sine)) * (1.0 / 128.0)
        for rows, cols, block in ((0, 0, kr), (0, 128, -ki), (128, 0, ki), (128, 128, kr)):
            top = block.astype(jnp.bfloat16)
            a_hi[f, rows:rows + 128, cols:cols + 128] = top
            a_lo[f, rows:rows + 128, cols:cols + 128] = (block - top.astype(jnp.float32)).astype(jnp.bfloat16)
        return carry

    lax.fori_loop(0, F, build, 0)

    forcing_out(1)
    c_copies[0].wait()
    by_row(part_l, 0, lf, other)
    c_copies[1].wait()
    by_row(part_u, 0, uf, other)
    c_copies[2].wait()
    by_row(part_p, 0, pf, other)

    def forward_column(n, carry):
        v = (-lf[0, 0, n], -lf[0, 1, n])
        pre[0, 0, n] = v[0]
        pre[0, 1, n] = v[1]

        def step(y, v):
            w = apply(lf, y, [v])[0]
            w = (-w[0], -w[1])
            pre[y, 0, n] = w[0]
            pre[y, 1, n] = w[1]
            return w

        v = lax.fori_loop(1, ROWS, step, v)
        tm[0, 0, n] = v[0]
        tm[0, 1, n] = v[1]
        return carry

    lax.fori_loop(0, F, forward_column, 0)

    def r_copy(ch, o, d):
        to = span_peer(o)
        c = core if d == 0 else other
        slot = core * S + me_s
        return remote(
            send_r.at[ch, to, c], driv.at[ch, slot], r_send.at[ch, c * S + to], r_recv.at[ch, slot], to, chip * 2 + c
        )

    def r_wait(ch, o, d):
        frm = span_peer(o)
        c = core if d == 0 else other
        slot = c * S + frm
        return remote(
            send_r.at[ch, frm, c], driv.at[ch, slot], r_send.at[ch, slot], r_recv.at[ch, slot], frm, chip * 2 + c
        )

    def r_local(ch):
        return pltpu.make_async_copy(send_r.at[ch, me_s, core], driv.at[ch, core * S + me_s], loc.at[2, ch])

    def filtered(ch, carry):
        f_local(ch).wait()

        def wait_f(o, carry):
            f_wait(ch, o).wait_recv()
            return carry

        lax.fori_loop(1, S, wait_f, 0)

        def field(f, carry):
            rhs = jnp.concatenate(
                [recv_f[ch, :, f, 0].reshape(128, 128), recv_f[ch, :, f, 1].reshape(128, 128)], axis=0
            )
            res = jnp.dot(a_hi[f], rhs, preferred_element_type=jnp.float32) + jnp.dot(
                a_lo[f], rhs, preferred_element_type=jnp.float32
            )
            re = res[:128].reshape(S, 2, 8, 128)
            im = res[128:].reshape(S, 2, 8, 128)
            top = jnp.max(jnp.maximum(jnp.abs(re), jnp.abs(im)), axis=2, keepdims=True)
            scale = jnp.maximum(top * 1.01, 1e-30).astype(jnp.bfloat16).astype(jnp.float32)
            scales[:, :, pl.ds(f, 1), :] = scale
            codes = jnp.concatenate([encode(re, scale), encode(im, scale)], axis=2)
            send_r[ch, :, :, f] = codes.astype(jnp.bfloat16)
            return carry

        lax.fori_loop(0, F, field, 0)
        send_r[ch, :, :, F] = jnp.concatenate([scales[...], scales[...]], axis=2).astype(jnp.bfloat16)
        r_local(ch).start()
        r_copy(ch, 0, 1).start()

        def start_r(o, carry):
            r_copy(ch, o, 0).start()
            r_copy(ch, o, 1).start()
            return carry

        lax.fori_loop(1, S, start_r, 0)
        return carry

    filtered(0, 0)

    def backward_column(n, carry):
        last = ROWS - 1
        v = (-uf[last, 0, n], -uf[last, 1, n])
        b = (pre[last, 0, n], pre[last, 1, n])

        def step(t, state):
            y = last - 1 - t
            v, b = state
            x, z = apply(uf, y, [v, b])
            return ((-x[0], -x[1]), (pre[y, 0, n] - z[0], pre[y, 1, n] - z[1]))

        v, b = lax.fori_loop(0, last, step, (v, b))
        tm[1, 0, n] = v[0]
        tm[1, 1, n] = v[1]
        tm[2, 0, n] = b[0]
        tm[2, 1, n] = b[1]
        return carry

    lax.fori_loop(0, F, backward_column, 0)

    def halves(p, q):
        axis = p.ndim - 1
        left = lax.broadcasted_iota(jnp.int32, p.shape, axis) < 64
        return (
            jnp.where(left, p, pltpu.roll(q, 64, axis)),
            jnp.where(left, pltpu.roll(p, 64, axis), q),
        )

    def pack_t(g, carry):
        at = (g // F) * 32 + lax.rem(g, F) * F
        d0, d1 = halves(tm[g // F, 0, lax.rem(g, F)], tm[g // F, 1, lax.rem(g, F)])
        for i in range(F):
            send_t[pl.ds(at + i, 8, stride=TR), :] = d0[i]
            send_t[pl.ds(8 * TR + at + i, 8, stride=TR), :] = d1[i]
        return carry

    lax.fori_loop(0, 3 * F, pack_t, 0)

    def code_transfers(n, carry):
        encode_blocks(send_t, code_t, 2 * n, 2, 3, 4, 25)
        return carry

    lax.fori_loop(0, K // 2, code_transfers, 0)

    def t_copy(o):
        to = wall_peer(o)
        return remote(code_t.at[to], got_t.at[chip], t_send.at[to], t_recv.at[chip], me_s, to * 2 + core)

    def t_wait(o):
        frm = wall_peer(o)
        return remote(code_t.at[frm], got_t.at[frm], t_send.at[frm], t_recv.at[frm], me_s, frm * 2 + core)

    t_local = pltpu.make_async_copy(code_t.at[chip], got_t.at[chip], loc.at[1, 0])
    t_local.start()

    def start_t(o, carry):
        t_copy(o).start()
        return carry

    lax.fori_loop(1, K, start_t, 0)

    filtered(1, 0)

    def a_copy(ch, o):
        to = wall_peer(o)
        return remote(
            code_a.at[ch * K + to], got_a.at[ch * K + chip], a_send.at[ch, to], a_recv.at[ch, chip], me_s, to * 2 + core
        )

    def a_wait(ch, o):
        frm = wall_peer(o)
        return remote(
            code_a.at[ch * K + frm], got_a.at[ch * K + frm], a_send.at[ch, frm], a_recv.at[ch, frm], me_s, frm * 2 + core
        )

    def a_local(ch):
        return pltpu.make_async_copy(code_a.at[ch * K + chip], got_a.at[ch * K + chip], loc.at[3, ch])

    zero = jnp.zeros((F, 8, 128), jnp.float32)

    def put(ref, y, state):
        for n in range(2):
            ref[y, n, 0] = state[n][0]
            ref[y, n, 1] = state[n][1]

    def get(ref, y):
        return [(ref[y, n, 0], ref[y, n, 1]) for n in range(2)]

    def local_solve(ch, carry):
        r_local(ch).wait()
        r_wait(ch, 0, 1).wait_recv()

        def wait_r(o, carry):
            r_wait(ch, o, 0).wait_recv()
            r_wait(ch, o, 1).wait_recv()
            return carry

        lax.fori_loop(1, S, wait_r, 0)

        def forward(y, state):
            base = (y // 4) * S + lax.rem(y, 4)
            drive = []
            for n in range(2):
                scale = driv[ch, base + 4 * n, F].astype(jnp.float32)
                parts = [
                    decode(driv[ch, base + 4 * n, f].astype(jnp.float32), scale[f:f + 1]) for f in range(F)
                ]
                drive.append((jnp.stack([x[:8] for x in parts]), jnp.stack([x[8:] for x in parts])))
            source = apply(pf, y, drive)
            put(src.at[ch], y, source)
            state = sub(source, apply(lf, y, state))
            put(sw, y, state)
            return state

        a = lax.fori_loop(0, ROWS, forward, [(zero, zero), (zero, zero)])

        def backward(t, state):
            y = ROWS - 2 - t
            return sub(get(sw, y), apply(uf, y, state))

        c = lax.fori_loop(0, ROWS - 1, backward, a)
        base = ch * (K * AR)
        for g, (p, q) in enumerate(((a[0][0], a[1][0]), (a[0][1], a[1][1]), (c[0][0], c[1][0]), (c[0][1], c[1][1]))):
            d0, d1 = halves(p, q)
            for i in range(F):
                send_a[pl.ds(base + g * F + i, 8, stride=AR), :] = d0[i]
                send_a[pl.ds(base + 8 * AR + g * F + i, 8, stride=AR), :] = d1[i]
        for n in range(2):
            encode_blocks(send_a, code_a, ch * K + 8 * n, 8, 1, 3, 20)
        a_local(ch).start()

        def start_a(o, carry):
            a_copy(ch, o).start()
            return carry

        lax.fori_loop(1, K, start_a, 0)
        return carry

    lax.fori_loop(0, 2, local_solve, 0)

    t_local.wait()

    def wait_t(o, carry):
        t_wait(o).wait_recv()
        return carry

    lax.fori_loop(1, K, wait_t, 0)

    def plain_transfers(n, carry):
        decode_blocks(got_t, recv_t, 2 * n, 2, 3, 4)
        return carry

    lax.fori_loop(0, K // 2, plain_transfers, 0)

    def expand(k, carry):
        for g in range(3 * F):
            rows = recv_t[pl.ds(k * TR + (g // F) * 32 + (g % F) * F, F), :]
            left = lax.broadcasted_iota(jnp.int32, rows.shape, 1) < 64
            turned = pltpu.roll(rows, 64, 1)
            te[k, g // F, 0, g % F, 0:F, :] = jnp.where(left, rows, turned)
            te[k, g // F, 1, g % F, 0:F, :] = jnp.where(left, turned, rows)
        return carry

    lax.fori_loop(0, K, expand, 0)

    def small(k, m, state, start):
        re, im = start
        for j in range(F):
            tr = te[k, m, 0, j, 0:F, :]
            ti = te[k, m, 1, j, 0:F, :]
            xr = state[0][j:j + 1]
            xi = state[1][j:j + 1]
            re = re + (tr * xr - ti * xi)
            im = im + (tr * xi + ti * xr)
        return re, im

    def s_copy(ch, o):
        to = wall_peer(o)
        return remote(
            code_s.at[ch * K + to], got_s.at[ch * K + chip], s_send.at[ch, to], s_recv.at[ch, chip], me_s, to * 2 + core
        )

    def s_wait(ch, o):
        frm = wall_peer(o)
        return remote(
            code_s.at[ch * K + frm], got_s.at[ch * K + frm], s_send.at[ch, frm], s_recv.at[ch, frm], me_s, frm * 2 + core
        )

    def s_local(ch):
        return pltpu.make_async_copy(code_s.at[ch * K + chip], got_s.at[ch * K + chip], loc.at[4, ch])

    flat = jnp.zeros((F, 128), jnp.float32)

    def owner_scan(ch, carry):
        a_local(ch).wait()

        def wait_a(o, carry):
            a_wait(ch, o).wait_recv()
            return carry

        lax.fori_loop(1, K, wait_a, 0)
        for n in range(2):
            decode_blocks(got_a, recv_a, ch * K + 8 * n, 8, 1, 3)

        def forward(k, state):
            base = (ch * K + k) * AR
            send_s[pl.ds(base, F), :] = state[0]
            send_s[pl.ds(base + F, F), :] = state[1]
            a = (recv_a[pl.ds(base, F), :], recv_a[pl.ds(base + F, F), :])
            c = (recv_a[pl.ds(base + 2 * F, F), :], recv_a[pl.ds(base + 3 * F, F), :])
            q = small(k, 2, state, c)
            qb[k, 0, 0:F, :] = q[0]
            qb[k, 1, 0:F, :] = q[1]
            return small(k, 0, state, a)

        lax.fori_loop(0, K, forward, (flat, flat))

        def backward(t, state):
            k = K - 1 - t
            base = (ch * K + k) * AR
            send_s[pl.ds(base + 2 * F, F), :] = state[0]
            send_s[pl.ds(base + 3 * F, F), :] = state[1]
            return small(k, 1, state, (qb[k, 0, 0:F, :], qb[k, 1, 0:F, :]))

        lax.fori_loop(0, K, backward, (flat, flat))
        for n in range(2):
            encode_blocks(send_s, code_s, ch * K + 8 * n, 8, 1, 3, 20)
        s_local(ch).start()

        def start_s(o, carry):
            s_copy(ch, o).start()
            return carry

        lax.fori_loop(1, K, start_s, 0)
        return carry

    lax.fori_loop(0, 2, owner_scan, 0)

    def o_copy(ch):
        return remote(
            resp.at[other, ch], out.at[:, pl.ds(2 * ch, 2), pl.ds(core * 32, 32), :],
            o_send.at[ch], o_recv.at[ch], me_s, partner,
        )

    def o_wait(ch):
        return remote(
            resp.at[other, ch], out.at[:, pl.ds(2 * ch, 2), pl.ds(other * 32, 32), :],
            o_send.at[ch], o_recv.at[ch], me_s, partner,
        )

    def o_local(ch):
        return pltpu.make_async_copy(
            resp.at[core, ch], out.at[:, pl.ds(2 * ch, 2), pl.ds(core * 32, 32), :], loc.at[5, ch]
        )

    def final(ch, carry):
        s_local(ch).wait()

        def wait_s(o, carry):
            s_wait(ch, o).wait_recv()
            return carry

        lax.fori_loop(1, K, wait_s, 0)
        for n in range(2):
            decode_blocks(got_s, recv_s, ch * K + 8 * n, 8, 1, 3)
        base = ch * (K * AR)

        def entering(g):
            e0 = jnp.stack([recv_s[pl.ds(base + g * F + i, 8, stride=AR), :] for i in range(F)])
            e1 = jnp.stack([recv_s[pl.ds(base + 8 * AR + g * F + i, 8, stride=AR), :] for i in range(F)])
            return halves(e0, e1)

        def pair(g):
            re = entering(g)
            im = entering(g + 1)
            return [(re[0], im[0]), (re[1], im[1])]

        def forward(y, state):
            state = sub(get(src.at[ch], y), apply(lf, y, state))
            put(sw, y, state)
            return state

        lax.fori_loop(0, ROWS, forward, pair(0))

        def backward(t, state):
            y = ROWS - 1 - t
            state = sub(get(sw, y), apply(uf, y, state))
            for n in range(2):
                for ri in range(2):
                    for i in range(F):
                        resp.at[y // 4, ch, ri * F + i, n][pl.ds(lax.rem(y, 4), 8, stride=4), :] = state[n][ri][i]
            return state

        lax.fori_loop(0, ROWS, backward, pair(2))
        o_local(ch).start()
        o_copy(ch).start()
        return carry

    lax.fori_loop(0, 2, final, 0)

    for ch in range(2):
        o_local(ch).wait()
        o_wait(ch).wait_recv()
        o_copy(ch).wait_send()
        r_copy(ch, 0, 1).wait_send()

        def end_span(o, carry):
            f_copy(ch, o).wait_send()
            r_copy(ch, o, 0).wait_send()
            r_copy(ch, o, 1).wait_send()
            return carry

        def end_wall(o, carry):
            a_copy(ch, o).wait_send()
            s_copy(ch, o).wait_send()
            return carry

        lax.fori_loop(1, S, end_span, 0)
        lax.fori_loop(1, K, end_wall, 0)

    def end_t(o, carry):
        t_copy(o).wait_send()
        return carry

    lax.fori_loop(1, K, end_t, 0)


def tables():
    n = np.arange(128)
    angle = (n[:, None] * n[None, :] % 128) * (2.0 * math.pi / 128)
    return np.stack([np.cos(angle), np.sin(angle)]).astype(np.float32)


def local(forcing, span_factor, pivot_inverse, step_lower, step_upper):
    f32, bf16 = jnp.float32, jnp.bfloat16
    dma = pltpu.SemaphoreType.DMA
    vm = pltpu.VMEM
    flat = [x.reshape(50, 64, 128) for x in (pivot_inverse, step_lower, step_upper)]
    coef = vm((ROWS, 2, F, F, 8, 128), f32)
    rows = vm((ROWS, 2, 2, F, 8, 128), f32)
    scratch = [
        vm((2 * F, 4, 64, 128), bf16), vm((F, 2, 128), f32), vm((2, 128, 128), f32),
        vm((50, 64, 128), bf16), vm((50, 64, 128), bf16), vm((50, 64, 128), bf16),
        vm((256, 128), f32),
        vm((S, 2, 8, 128), f32),
        vm((2, S, F, 2, 16, 128), bf16),
        vm((2, S, F, 2, 16, 128), bf16),
        vm((50, 32, 128), bf16), vm((50, 32, 128), bf16), vm((50, 32, 128), bf16),
        coef, coef, coef, coef,
        vm((3, 2, F, F, 8, 128), f32),
        vm((F, 256, 256), bf16), vm((F, 256, 256), bf16),
        vm((2, S, 2, F + 1, 16, 128), bf16),
        vm((2, 2 * S, F + 1, 16, 128), bf16),
        vm((K * TR, 128), f32), vm((K * TR, 128), f32),
        vm((K, 3, 2, F, 8, 128), f32),
        vm((2 * K * AR, 128), f32), vm((2 * K * AR, 128), f32),
        vm((2 * K * AR, 128), f32), vm((2 * K * AR, 128), f32),
        vm((K, 12, 8, 128), bf16), vm((K, 12, 8, 128), bf16),
        vm((2 * K, 3, 8, 128), bf16), vm((2 * K, 3, 8, 128), bf16),
        vm((2 * K, 3, 8, 128), bf16), vm((2 * K, 3, 8, 128), bf16),
        vm((2, ROWS, 2, 2, F, 8, 128), f32),
        rows,
        vm((K, 2, 8, 128), f32),
        vm((2, 2, 2 * F, 2, 32, 128), f32),
        dma((3,)), dma((3,)),
        dma((2, S)), dma((2, S)),
        dma((2, 2 * S)), dma((2, 2 * S)),
        dma((K,)), dma((K,)),
        dma((2, K)), dma((2, K)),
        dma((2, K)), dma((2, K)),
        dma((2,)), dma((2,)),
        dma((6, 2)),
        dma((6,)),
    ]
    out = pl.pallas_call(
        kernel,
        out_shape=jax.ShapeDtypeStruct((2 * F, 4, 64, 128), f32),
        in_specs=[pl.BlockSpec(memory_space=pl.ANY)] * 6,
        out_specs=pl.BlockSpec(memory_space=pl.ANY),
        scratch_shapes=scratch,
        compiler_params=pltpu.CompilerParams(
            collective_id=0, has_side_effects=True, vmem_limit_bytes=56 << 20
        ),
    )(
        forcing.reshape(2 * F, 4, 64, 128),
        jnp.swapaxes(span_factor, 0, 1),
        jnp.asarray(tables()),
        *flat,
    )
    return out.reshape(2, F, 4, 16, 4, 128)


def solution(mesh):
    placed = P(None, None, None, "span", "wall", None)
    return jax.shard_map(
        local,
        mesh=mesh,
        in_specs=(placed, P(), placed, placed, placed),
        out_specs=placed,
        check_vma=False,
    )
```

```python
import functools
import math

import jax
import jax.numpy as jnp
import numpy as np
from jax import lax
from jax.experimental import pallas as pl
from jax.experimental.pallas import tpu as pltpu
from jax.sharding import PartitionSpec as P

MESH = pl.DeviceIdType.MESH
F = 5
S = 8
K = 16
ROWS = 8
TR = 96
AR = 24
HI = lax.Precision.HIGHEST
LEVELS = 29900.0
SHIFT = 117.0


def encode(x, scale):
    y = x * (LEVELS / scale)
    n = jnp.floor(jnp.abs(y) + 0.5)
    e = jnp.floor(n * (1.0 / 128.0))
    v = (1.0 + (n - 128.0 * e) * (1.0 / 128.0)) * jnp.exp2(e - SHIFT)
    return jnp.where(y < 0.0, -v, v)


def decode(v, scale):
    a = jnp.abs(v)
    e = jnp.floor(jnp.log2(a) + 0.002)
    n = 128.0 * (e + (SHIFT - 1.0)) + 128.0 * (a * jnp.exp2(-e))
    return jnp.where(v < 0.0, -n, n) * (scale * (1.0 / LEVELS))


def encode_blocks(src, dst, first, count, parts, tiles, used):
    rows = parts * tiles * 8
    x = src[pl.ds(pl.multiple_of(first * rows, 8), count * rows), :].reshape(count * parts, tiles, 8, 128)
    place = lax.broadcasted_iota(jnp.int32, x.shape, 1) * 8 + lax.broadcasted_iota(jnp.int32, x.shape, 2)
    good = place < used
    x = jnp.where(good, x, 0.0)
    top = jnp.max(jnp.max(jnp.abs(x), axis=1, keepdims=True), axis=2, keepdims=True)
    scale = jnp.maximum(top * 1.01, 1e-30).astype(jnp.bfloat16).astype(jnp.float32)
    code = jnp.where(good, encode(x, scale), scale).astype(jnp.bfloat16)
    dst[pl.ds(first, count)] = code.reshape(count, parts * tiles, 8, 128)


def decode_blocks(src, dst, first, count, parts, tiles):
    rows = parts * tiles * 8
    code = src[pl.ds(first, count)].astype(jnp.float32).reshape(count * parts, tiles, 8, 128)
    x = decode(code, code[:, tiles - 1:, 7:, :])
    dst[pl.ds(pl.multiple_of(first * rows, 8), count * rows), :] = x.reshape(count * rows, 128)


def apply(coef, y, vectors):
    out = [None] * len(vectors)
    for j in range(F):
        cr = coef[y, 0, j]
        ci = coef[y, 1, j]
        for n, (vr, vi) in enumerate(vectors):
            xr = vr[j][None]
            xi = vi[j][None]
            re = cr * xr - ci * xi
            im = cr * xi + ci * xr
            out[n] = (re, im) if out[n] is None else (out[n][0] + re, out[n][1] + im)
    return out


def sub(a, b):
    return [(x[0] - y[0], x[1] - y[1]) for x, y in zip(a, b)]


def kernel(
    forcing_in, factor_in, table_in, piv_in, low_in, upp_in, out,
    forcing, factor, table, piv, low, upp, tmp, line, scales, send_f, recv_f, part_p, part_l, part_u, pf, lf, uf, pre, tm, a_hi, a_lo,
    send_r, driv, send_t, recv_t, te, send_a, recv_a, send_s, recv_s,
    code_t, got_t, code_a, got_a, code_s, got_s, src, sw, qb, resp,
    c_send, c_recv, f_send, f_recv, r_send, r_recv, t_send, t_recv, a_send, a_recv, s_send, s_recv,
    o_send, o_recv, loc, load,
):
    me_s = lax.axis_index("span")
    me_w = lax.axis_index("wall")
    core = lax.rem(me_w, 2)
    chip = me_w // 2
    other = 1 - core
    partner = chip * 2 + other

    def span_peer(o):
        return lax.rem(me_s + o, S)

    def wall_peer(o):
        return lax.rem(chip + o, K)

    loads = [
        pltpu.make_async_copy(a, b, load.at[n])
        for n, (a, b) in enumerate(
            (
                (forcing_in, forcing), (low_in, low), (upp_in, upp), (piv_in, piv),
                (factor_in, factor), (table_in, table),
            )
        )
    ]
    for copy in loads:
        copy.start()

    barrier = pltpu.get_barrier_semaphore()

    def greet(s, w):
        pl.semaphore_signal(barrier, inc=1, device_id=(s, w), device_id_type=MESH)

    def greet_span(o, carry):
        greet(span_peer(o), me_w)
        greet(span_peer(o), partner)
        return carry

    def greet_wall(o, carry):
        greet(me_s, wall_peer(o) * 2 + core)
        return carry

    lax.fori_loop(1, S, greet_span, 0)
    lax.fori_loop(1, K, greet_wall, 0)
    greet(me_s, partner)

    def regroup(g, carry):
        for col in range(4):
            tmp[pl.ds(col * 64, 64), :] = forcing[g, col].astype(jnp.float32)
        for col in range(4):
            for y in range(4):
                piece = tmp[pl.ds(col * 64 + y, 16, stride=4), :].astype(jnp.bfloat16)
                send_f[col // 2, (col % 2) * 4 + y, lax.rem(g, F), g // F] = piece
        return carry

    loads[0].wait()
    lax.fori_loop(0, 2 * F, regroup, 0)

    pl.semaphore_wait(barrier, 2 * S - 1 + K - 1)

    def remote(src_ref, dst_ref, ss, rs, s, w):
        return pltpu.make_async_remote_copy(
            src_ref=src_ref, dst_ref=dst_ref, send_sem=ss, recv_sem=rs,
            device_id=(s, w), device_id_type=MESH,
        )

    def f_copy(ch, o):
        to = span_peer(o)
        return remote(send_f.at[ch, to], recv_f.at[ch, me_s], f_send.at[ch, to], f_recv.at[ch, me_s], to, me_w)

    def f_wait(ch, o):
        frm = span_peer(o)
        return remote(send_f.at[ch, frm], recv_f.at[ch, frm], f_send.at[ch, frm], f_recv.at[ch, frm], frm, me_w)

    def f_local(ch):
        return pltpu.make_async_copy(send_f.at[ch, me_s], recv_f.at[ch, me_s], loc.at[0, ch])

    def c_copy(n, ref, part):
        return remote(ref.at[:, pl.ds(other * 32, 32), :], part, c_send.at[n], c_recv.at[n], me_s, partner)

    c_copies = [c_copy(0, low_in, part_l), c_copy(1, upp_in, part_u), c_copy(2, piv_in, part_p)]

    def forcing_out(ch):
        f_local(ch).start()

        def start_f(o, carry):
            f_copy(ch, o).start()
            return carry

        lax.fori_loop(1, S, start_f, 0)

    forcing_out(0)
    for copy in c_copies:
        copy.start()
    for copy in loads[1:]:
        copy.wait()

    def by_row(ref, first, dst, at):
        def step(g, carry):
            for j in range(F):
                tmp[pl.ds(j * 32, 32), :] = ref[g * F + j, pl.ds(first, 32), :].astype(jnp.float32)
            for j in range(F):
                for y in range(4):
                    dst[at * 4 + y, g // F, j, lax.rem(g, F)] = tmp[pl.ds(j * 32 + y, 8, stride=4), :]
            return carry

        lax.fori_loop(0, 2 * F, step, 0)

    mine = pl.multiple_of(core * 32, 32)
    by_row(low, mine, lf, core)
    by_row(upp, mine, uf, core)
    by_row(piv, mine, pf, core)
    dot = functools.partial(jnp.dot, precision=HI, preferred_element_type=jnp.float32)
    for f in range(F):
        line[0, f:f + 1, :] = factor[f, 0:1, :]
        line[1, f:f + 1, :] = factor[f, 1:2, :]
    factor_re = line[0, 0:F, :]
    factor_im = line[1, 0:F, :]
    first_re = (dot(factor_re, table[0]) + dot(factor_im, table[1])) * (1.0 / 128.0)
    first_im = (dot(factor_im, table[0]) - dot(factor_re, table[1])) * (1.0 / 128.0)
    line[0, 0:F, :] = first_re
    line[1, 0:F, :] = first_im

    def build(f, carry):
        turn = lambda row: pltpu.roll(jnp.broadcast_to(row, (128, 128)), 0, 1, stride=1, stride_axis=0)
        kr = turn(line[0, pl.ds(f, 1), :])
        ki = turn(line[1, pl.ds(f, 1), :])
        for rows, cols, block in ((0, 0, kr), (0, 128, -ki), (128, 0, ki), (128, 128, kr)):
            top = block.astype(jnp.bfloat16)
            a_hi[f, rows:rows + 128, cols:cols + 128] = top
            a_lo[f, rows:rows + 128, cols:cols + 128] = (block - top.astype(jnp.float32)).astype(jnp.bfloat16)
        return carry

    lax.fori_loop(0, F, build, 0)

    forcing_out(1)
    c_copies[0].wait()
    by_row(part_l, 0, lf, other)
    c_copies[1].wait()
    by_row(part_u, 0, uf, other)
    c_copies[2].wait()
    by_row(part_p, 0, pf, other)

    def forward_column(n, carry):
        v = (-lf[0, 0, n], -lf[0, 1, n])
        pre[0, 0, n] = v[0]
        pre[0, 1, n] = v[1]

        def step(y, v):
            w = apply(lf, y, [v])[0]
            w = (-w[0], -w[1])
            pre[y, 0, n] = w[0]
            pre[y, 1, n] = w[1]
            return w

        v = lax.fori_loop(1, ROWS, step, v)
        tm[0, 0, n] = v[0]
        tm[0, 1, n] = v[1]
        return carry

    lax.fori_loop(0, F, forward_column, 0)

    def r_copy(ch, o, d):
        to = span_peer(o)
        c = core if d == 0 else other
        slot = core * S + me_s
        return remote(
            send_r.at[ch, to, c], driv.at[ch, slot], r_send.at[ch, c * S + to], r_recv.at[ch, slot], to, chip * 2 + c
        )

    def r_wait(ch, o, d):
        frm = span_peer(o)
        c = core if d == 0 else other
        slot = c * S + frm
        return remote(
            send_r.at[ch, frm, c], driv.at[ch, slot], r_send.at[ch, slot], r_recv.at[ch, slot], frm, chip * 2 + c
        )

    def r_local(ch):
        return pltpu.make_async_copy(send_r.at[ch, me_s, core], driv.at[ch, core * S + me_s], loc.at[2, ch])

    def filtered(ch, carry):
        f_local(ch).wait()

        def wait_f(o, carry):
            f_wait(ch, o).wait_recv()
            return carry

        lax.fori_loop(1, S, wait_f, 0)

        def field(f, carry):
            rhs = jnp.concatenate(
                [recv_f[ch, :, f, 0].reshape(128, 128), recv_f[ch, :, f, 1].reshape(128, 128)], axis=0
            )
            res = jnp.dot(a_hi[f], rhs, preferred_element_type=jnp.float32) + jnp.dot(
                a_lo[f], rhs, preferred_element_type=jnp.float32
            )
            re = res[:128].reshape(S, 2, 8, 128)
            im = res[128:].reshape(S, 2, 8, 128)
            top = jnp.max(jnp.maximum(jnp.abs(re), jnp.abs(im)), axis=2, keepdims=True)
            scale = jnp.maximum(top * 1.01, 1e-30).astype(jnp.bfloat16).astype(jnp.float32)
            scales[:, :, pl.ds(f, 1), :] = scale
            send_r[ch, :, :, f] = encode(re, scale).astype(jnp.bfloat16)
            send_r[ch, :, :, F + f] = encode(im, scale).astype(jnp.bfloat16)
            return carry

        lax.fori_loop(0, F, field, 0)
        send_r[ch, :, :, 2 * F] = scales[...].astype(jnp.bfloat16)
        r_local(ch).start()
        r_copy(ch, 0, 1).start()

        def start_r(o, carry):
            r_copy(ch, o, 0).start()
            r_copy(ch, o, 1).start()
            return carry

        lax.fori_loop(1, S, start_r, 0)
        return carry

    def backward_column(n, carry):
        last = ROWS - 1
        v = (-uf[last, 0, n], -uf[last, 1, n])
        b = (pre[last, 0, n], pre[last, 1, n])

        def step(t, state):
            y = last - 1 - t
            v, b = state
            x, z = apply(uf, y, [v, b])
            return ((-x[0], -x[1]), (pre[y, 0, n] - z[0], pre[y, 1, n] - z[1]))

        v, b = lax.fori_loop(0, last, step, (v, b))
        tm[1, 0, n] = v[0]
        tm[1, 1, n] = v[1]
        tm[2, 0, n] = b[0]
        tm[2, 1, n] = b[1]
        return carry

    lax.fori_loop(0, 2, backward_column, 0)
    filtered(0, 0)

    lax.fori_loop(2, F, backward_column, 0)

    def halves(p, q):
        axis = p.ndim - 1
        left = lax.broadcasted_iota(jnp.int32, p.shape, axis) < 64
        return (
            jnp.where(left, p, pltpu.roll(q, 64, axis)),
            jnp.where(left, pltpu.roll(p, 64, axis), q),
        )

    def pack_t(g, carry):
        at = (g // F) * 32 + lax.rem(g, F) * F
        d0, d1 = halves(tm[g // F, 0, lax.rem(g, F)], tm[g // F, 1, lax.rem(g, F)])
        for i in range(F):
            send_t[pl.ds(at + i, 8, stride=TR), :] = d0[i]
            send_t[pl.ds(8 * TR + at + i, 8, stride=TR), :] = d1[i]
        return carry

    lax.fori_loop(0, 3 * F, pack_t, 0)

    def code_transfers(n, carry):
        encode_blocks(send_t, code_t, 2 * n, 2, 3, 4, 25)
        return carry

    lax.fori_loop(0, K // 2, code_transfers, 0)

    def t_copy(o):
        to = wall_peer(o)
        return remote(code_t.at[to], got_t.at[chip], t_send.at[to], t_recv.at[chip], me_s, to * 2 + core)

    def t_wait(o):
        frm = wall_peer(o)
        return remote(code_t.at[frm], got_t.at[frm], t_send.at[frm], t_recv.at[frm], me_s, frm * 2 + core)

    t_local = pltpu.make_async_copy(code_t.at[chip], got_t.at[chip], loc.at[1, 0])
    t_local.start()

    def start_t(o, carry):
        t_copy(o).start()
        return carry

    lax.fori_loop(1, K, start_t, 0)

    filtered(1, 0)

    def a_copy(ch, o):
        to = wall_peer(o)
        return remote(
            code_a.at[ch * K + to], got_a.at[ch * K + chip], a_send.at[ch, to], a_recv.at[ch, chip], me_s, to * 2 + core
        )

    def a_wait(ch, o):
        frm = wall_peer(o)
        return remote(
            code_a.at[ch * K + frm], got_a.at[ch * K + frm], a_send.at[ch, frm], a_recv.at[ch, frm], me_s, frm * 2 + core
        )

    def a_local(ch):
        return pltpu.make_async_copy(code_a.at[ch * K + chip], got_a.at[ch * K + chip], loc.at[3, ch])

    zero = jnp.zeros((F, 8, 128), jnp.float32)

    def put(ref, y, state):
        for n in range(2):
            ref[y, n, 0] = state[n][0]
            ref[y, n, 1] = state[n][1]

    def get(ref, y):
        return [(ref[y, n, 0], ref[y, n, 1]) for n in range(2)]

    def local_solve(ch, carry):
        r_local(ch).wait()
        r_wait(ch, 0, 1).wait_recv()

        def wait_r(o, carry):
            r_wait(ch, o, 0).wait_recv()
            r_wait(ch, o, 1).wait_recv()
            return carry

        lax.fori_loop(1, S, wait_r, 0)

        def forward(y, state):
            base = (y // 4) * S + lax.rem(y, 4)
            drive = []
            for n in range(2):
                code = driv[ch, base + 4 * n].astype(jnp.float32)
                scale = jnp.stack([jnp.broadcast_to(code[2 * F, f:f + 1], (8, 128)) for f in range(F)])
                drive.append((decode(code[:F], scale), decode(code[F:2 * F], scale)))
            source = apply(pf, y, drive)
            put(src.at[ch], y, source)
            state = sub(source, apply(lf, y, state))
            put(sw, y, state)
            return state

        a = lax.fori_loop(0, ROWS, forward, [(zero, zero), (zero, zero)])

        def backward(t, state):
            y = ROWS - 2 - t
            return sub(get(sw, y), apply(uf, y, state))

        c = lax.fori_loop(0, ROWS - 1, backward, a)
        base = ch * (K * AR)
        for g, (p, q) in enumerate(((a[0][0], a[1][0]), (a[0][1], a[1][1]), (c[0][0], c[1][0]), (c[0][1], c[1][1]))):
            d0, d1 = halves(p, q)
            for i in range(F):
                send_a[pl.ds(base + g * F + i, 8, stride=AR), :] = d0[i]
                send_a[pl.ds(base + 8 * AR + g * F + i, 8, stride=AR), :] = d1[i]
        for n in range(2):
            encode_blocks(send_a, code_a, ch * K + 8 * n, 8, 1, 3, 20)
        a_local(ch).start()

        def start_a(o, carry):
            a_copy(ch, o).start()
            return carry

        lax.fori_loop(1, K, start_a, 0)
        return carry

    lax.fori_loop(0, 2, local_solve, 0)

    t_local.wait()

    def wait_t(o, carry):
        t_wait(o).wait_recv()
        return carry

    lax.fori_loop(1, K, wait_t, 0)

    def plain_transfers(n, carry):
        decode_blocks(got_t, recv_t, 2 * n, 2, 3, 4)
        return carry

    lax.fori_loop(0, K // 2, plain_transfers, 0)

    def expand(k, carry):
        for g in range(3 * F):
            rows = recv_t[pl.ds(k * TR + (g // F) * 32 + (g % F) * F, F), :]
            left = lax.broadcasted_iota(jnp.int32, rows.shape, 1) < 64
            turned = pltpu.roll(rows, 64, 1)
            te[k, g // F, 0, g % F, 0:F, :] = jnp.where(left, rows, turned)
            te[k, g // F, 1, g % F, 0:F, :] = jnp.where(left, turned, rows)
        return carry

    lax.fori_loop(0, K, expand, 0)

    def small(k, m, state, start):
        re, im = start
        for j in range(F):
            tr = te[k, m, 0, j, 0:F, :]
            ti = te[k, m, 1, j, 0:F, :]
            xr = state[0][j:j + 1]
            xi = state[1][j:j + 1]
            re = re + (tr * xr - ti * xi)
            im = im + (tr * xi + ti * xr)
        return re, im

    def s_copy(ch, o):
        to = wall_peer(o)
        return remote(
            code_s.at[ch * K + to], got_s.at[ch * K + chip], s_send.at[ch, to], s_recv.at[ch, chip], me_s, to * 2 + core
        )

    def s_wait(ch, o):
        frm = wall_peer(o)
        return remote(
            code_s.at[ch * K + frm], got_s.at[ch * K + frm], s_send.at[ch, frm], s_recv.at[ch, frm], me_s, frm * 2 + core
        )

    def s_local(ch):
        return pltpu.make_async_copy(code_s.at[ch * K + chip], got_s.at[ch * K + chip], loc.at[4, ch])

    flat = jnp.zeros((F, 128), jnp.float32)

    def owner_scan(ch, carry):
        a_local(ch).wait()

        def wait_a(o, carry):
            a_wait(ch, o).wait_recv()
            return carry

        lax.fori_loop(1, K, wait_a, 0)
        for n in range(2):
            decode_blocks(got_a, recv_a, ch * K + 8 * n, 8, 1, 3)

        def forward(k, state):
            base = (ch * K + k) * AR
            send_s[pl.ds(base, F), :] = state[0]
            send_s[pl.ds(base + F, F), :] = state[1]
            a = (recv_a[pl.ds(base, F), :], recv_a[pl.ds(base + F, F), :])
            c = (recv_a[pl.ds(base + 2 * F, F), :], recv_a[pl.ds(base + 3 * F, F), :])
            q = small(k, 2, state, c)
            qb[k, 0, 0:F, :] = q[0]
            qb[k, 1, 0:F, :] = q[1]
            return small(k, 0, state, a)

        lax.fori_loop(0, K, forward, (flat, flat))

        def backward(t, state):
            k = K - 1 - t
            base = (ch * K + k) * AR
            send_s[pl.ds(base + 2 * F, F), :] = state[0]
            send_s[pl.ds(base + 3 * F, F), :] = state[1]
            return small(k, 1, state, (qb[k, 0, 0:F, :], qb[k, 1, 0:F, :]))

        lax.fori_loop(0, K, backward, (flat, flat))
        for n in range(2):
            encode_blocks(send_s, code_s, ch * K + 8 * n, 8, 1, 3, 20)
        s_local(ch).start()

        def start_s(o, carry):
            s_copy(ch, o).start()
            return carry

        lax.fori_loop(1, K, start_s, 0)
        return carry

    lax.fori_loop(0, 2, owner_scan, 0)

    def o_copy(ch):
        return remote(
            resp.at[other, ch], out.at[:, pl.ds(2 * ch, 2), pl.ds(core * 32, 32), :],
            o_send.at[ch], o_recv.at[ch], me_s, partner,
        )

    def o_wait(ch):
        return remote(
            resp.at[other, ch], out.at[:, pl.ds(2 * ch, 2), pl.ds(other * 32, 32), :],
            o_send.at[ch], o_recv.at[ch], me_s, partner,
        )

    def o_local(ch):
        return pltpu.make_async_copy(
            resp.at[core, ch], out.at[:, pl.ds(2 * ch, 2), pl.ds(core * 32, 32), :], loc.at[5, ch]
        )

    def final(ch, carry):
        s_local(ch).wait()

        def wait_s(o, carry):
            s_wait(ch, o).wait_recv()
            return carry

        lax.fori_loop(1, K, wait_s, 0)
        for n in range(2):
            decode_blocks(got_s, recv_s, ch * K + 8 * n, 8, 1, 3)
        base = ch * (K * AR)

        def entering(g):
            e0 = jnp.stack([recv_s[pl.ds(base + g * F + i, 8, stride=AR), :] for i in range(F)])
            e1 = jnp.stack([recv_s[pl.ds(base + 8 * AR + g * F + i, 8, stride=AR), :] for i in range(F)])
            return halves(e0, e1)

        def pair(g):
            re = entering(g)
            im = entering(g + 1)
            return [(re[0], im[0]), (re[1], im[1])]

        def forward(y, state):
            state = sub(get(src.at[ch], y), apply(lf, y, state))
            put(sw, y, state)
            return state

        lax.fori_loop(0, ROWS, forward, pair(0))

        def backward(t, state):
            y = ROWS - 1 - t
            state = sub(get(sw, y), apply(uf, y, state))
            for n in range(2):
                for ri in range(2):
                    for i in range(F):
                        resp.at[y // 4, ch, ri * F + i, n][pl.ds(lax.rem(y, 4), 8, stride=4), :] = state[n][ri][i]
            return state

        lax.fori_loop(0, ROWS, backward, pair(2))
        o_local(ch).start()
        o_copy(ch).start()
        return carry

    lax.fori_loop(0, 2, final, 0)

    for ch in range(2):
        o_local(ch).wait()
        o_wait(ch).wait_recv()
        o_copy(ch).wait_send()
        r_copy(ch, 0, 1).wait_send()

        def end_span(o, carry):
            f_copy(ch, o).wait_send()
            r_copy(ch, o, 0).wait_send()
            r_copy(ch, o, 1).wait_send()
            return carry

        def end_wall(o, carry):
            a_copy(ch, o).wait_send()
            s_copy(ch, o).wait_send()
            return carry

        lax.fori_loop(1, S, end_span, 0)
        lax.fori_loop(1, K, end_wall, 0)

    def end_t(o, carry):
        t_copy(o).wait_send()
        return carry

    lax.fori_loop(1, K, end_t, 0)


def tables():
    n = np.arange(128)
    angle = (n[:, None] * n[None, :] % 128) * (2.0 * math.pi / 128)
    return np.stack([np.cos(angle), np.sin(angle)]).astype(np.float32)


def local(forcing, span_factor, pivot_inverse, step_lower, step_upper):
    f32, bf16 = jnp.float32, jnp.bfloat16
    dma = pltpu.SemaphoreType.DMA
    vm = pltpu.VMEM
    flat = [x.reshape(50, 64, 128) for x in (pivot_inverse, step_lower, step_upper)]
    coef = vm((ROWS, 2, F, F, 8, 128), f32)
    rows = vm((ROWS, 2, 2, F, 8, 128), f32)
    scratch = [
        vm((2 * F, 4, 64, 128), bf16), vm((F, 2, 128), f32), vm((2, 128, 128), f32),
        vm((50, 64, 128), bf16), vm((50, 64, 128), bf16), vm((50, 64, 128), bf16),
        vm((256, 128), f32),
        vm((2, 8, 128), f32),
        vm((S, 2, 8, 128), f32),
        vm((2, S, F, 2, 16, 128), bf16),
        vm((2, S, F, 2, 16, 128), bf16),
        vm((50, 32, 128), bf16), vm((50, 32, 128), bf16), vm((50, 32, 128), bf16),
        coef, coef, coef, coef,
        vm((3, 2, F, F, 8, 128), f32),
        vm((F, 256, 256), bf16), vm((F, 256, 256), bf16),
        vm((2, S, 2, 2 * F + 1, 8, 128), bf16),
        vm((2, 2 * S, 2 * F + 1, 8, 128), bf16),
        vm((K * TR, 128), f32), vm((K * TR, 128), f32),
        vm((K, 3, 2, F, 8, 128), f32),
        vm((2 * K * AR, 128), f32), vm((2 * K * AR, 128), f32),
        vm((2 * K * AR, 128), f32), vm((2 * K * AR, 128), f32),
        vm((K, 12, 8, 128), bf16), vm((K, 12, 8, 128), bf16),
        vm((2 * K, 3, 8, 128), bf16), vm((2 * K, 3, 8, 128), bf16),
        vm((2 * K, 3, 8, 128), bf16), vm((2 * K, 3, 8, 128), bf16),
        vm((2, ROWS, 2, 2, F, 8, 128), f32),
        rows,
        vm((K, 2, 8, 128), f32),
        vm((2, 2, 2 * F, 2, 32, 128), f32),
        dma((3,)), dma((3,)),
        dma((2, S)), dma((2, S)),
        dma((2, 2 * S)), dma((2, 2 * S)),
        dma((K,)), dma((K,)),
        dma((2, K)), dma((2, K)),
        dma((2, K)), dma((2, K)),
        dma((2,)), dma((2,)),
        dma((6, 2)),
        dma((6,)),
    ]
    out = pl.pallas_call(
        kernel,
        out_shape=jax.ShapeDtypeStruct((2 * F, 4, 64, 128), f32),
        in_specs=[pl.BlockSpec(memory_space=pltpu.HBM)] * 6,
        out_specs=pl.BlockSpec(memory_space=pl.ANY),
        scratch_shapes=scratch,
        compiler_params=pltpu.CompilerParams(
            collective_id=0, has_side_effects=True, vmem_limit_bytes=34 << 20
        ),
    )(
        *[
            pltpu.with_memory_space_constraint(x, pltpu.HBM)
            for x in (
                forcing.reshape(2 * F, 4, 64, 128),
                jnp.swapaxes(span_factor, 0, 1),
                jnp.asarray(tables()),
                *flat,
            )
        ]
    )
    return out.reshape(2, F, 4, 16, 4, 128)


def solution(mesh):
    placed = P(None, None, None, "span", "wall", None)
    return jax.shard_map(
        local,
        mesh=mesh,
        in_specs=(placed, P(), placed, placed, placed),
        out_specs=placed,
        check_vma=False,
    )
```

```python
import functools
import math

import jax
import jax.numpy as jnp
import numpy as np
from jax import lax
from jax.experimental import pallas as pl
from jax.experimental.pallas import tpu as pltpu
from jax.sharding import PartitionSpec as P

MESH = pl.DeviceIdType.MESH
F = 5
S = 8
K = 16
ROWS = 8
TR = 96
AR = 24
HI = lax.Precision.HIGHEST
LEVELS = 29900.0
SHIFT = 117.0


def encode(x, scale):
    y = x * (LEVELS / scale)
    n = jnp.floor(jnp.abs(y) + 0.5)
    e = jnp.floor(n * (1.0 / 128.0))
    v = (1.0 + (n - 128.0 * e) * (1.0 / 128.0)) * jnp.exp2(e - SHIFT)
    return jnp.where(y < 0.0, -v, v)


def decode(v, scale):
    a = jnp.abs(v)
    e = jnp.floor(jnp.log2(a) + 0.002)
    n = 128.0 * (e + (SHIFT - 1.0)) + 128.0 * (a * jnp.exp2(-e))
    return jnp.where(v < 0.0, -n, n) * (scale * (1.0 / LEVELS))


def encode_blocks(src, dst, first, count, parts, tiles, used):
    rows = parts * tiles * 8
    x = src[pl.ds(pl.multiple_of(first * rows, 8), count * rows), :].reshape(count * parts, tiles, 8, 128)
    place = lax.broadcasted_iota(jnp.int32, x.shape, 1) * 8 + lax.broadcasted_iota(jnp.int32, x.shape, 2)
    good = place < used
    x = jnp.where(good, x, 0.0)
    top = jnp.max(jnp.max(jnp.abs(x), axis=1, keepdims=True), axis=2, keepdims=True)
    scale = jnp.maximum(top * 1.01, 1e-30).astype(jnp.bfloat16).astype(jnp.float32)
    code = jnp.where(good, encode(x, scale), scale).astype(jnp.bfloat16)
    dst[pl.ds(first, count)] = code.reshape(count, parts * tiles, 8, 128)


def decode_blocks(src, dst, first, count, parts, tiles):
    rows = parts * tiles * 8
    code = src[pl.ds(first, count)].astype(jnp.float32).reshape(count * parts, tiles, 8, 128)
    x = decode(code, code[:, tiles - 1:, 7:, :])
    dst[pl.ds(pl.multiple_of(first * rows, 8), count * rows), :] = x.reshape(count * rows, 128)


def apply(coef, y, vectors):
    out = [None] * len(vectors)
    for j in range(F):
        cr = coef[y, 0, j]
        ci = coef[y, 1, j]
        for n, (vr, vi) in enumerate(vectors):
            xr = vr[j][None]
            xi = vi[j][None]
            re = cr * xr - ci * xi
            im = cr * xi + ci * xr
            out[n] = (re, im) if out[n] is None else (out[n][0] + re, out[n][1] + im)
    return out


def sub(a, b):
    return [(x[0] - y[0], x[1] - y[1]) for x, y in zip(a, b)]


def kernel(
    forcing_in, factor_in, table_in, piv_in, low_in, upp_in, out,
    forcing, factor, table, piv, low, upp, tmp, line, scales, send_f, recv_f, part_p, part_l, part_u, pf, lf, uf, pre, tm, a_hi, a_lo,
    send_r, driv, send_t, recv_t, te, send_a, recv_a, send_s, recv_s,
    code_t, got_t, code_a, got_a, code_s, got_s, src, sw, qb, resp,
    c_send, c_recv, f_send, f_recv, r_send, r_recv, t_send, t_recv, a_send, a_recv, s_send, s_recv,
    o_send, o_recv, loc, load,
):
    me_s = lax.axis_index("span")
    me_w = lax.axis_index("wall")
    core = lax.rem(me_w, 2)
    chip = me_w // 2
    other = 1 - core
    partner = chip * 2 + other

    def ordered(i, n, first):
        step = (i + 1) // 2
        return lax.rem(n // 2 + n + jnp.where(lax.rem(i, 2) == first, step, -step), n)

    def span_peer(o):
        y = lax.rem(me_s // 4 + 1 - lax.rem(o, 2), 2)
        x = lax.rem(lax.rem(me_s, 4) + ordered(o // 2, 4, 0), 4)
        return y * 4 + x

    def wall_peer(o):
        y = lax.rem(chip // 8 + 1 - o // 8, 2)
        z = lax.rem(lax.rem(chip, 8) + ordered(lax.rem(o, 8), 8, 1), 8)
        return y * 8 + z

    loads = [
        pltpu.make_async_copy(a, b, load.at[n])
        for n, (a, b) in enumerate(
            (
                (forcing_in, forcing), (low_in, low), (upp_in, upp), (piv_in, piv),
                (factor_in, factor), (table_in, table),
            )
        )
    ]
    loads[0].start()

    barrier = pltpu.get_barrier_semaphore()

    def greet(s, w):
        pl.semaphore_signal(barrier, inc=1, device_id=(s, w), device_id_type=MESH)

    def greet_span(o, carry):
        greet(span_peer(o), me_w)
        greet(span_peer(o), partner)
        return carry

    def greet_wall(o, carry):
        greet(me_s, wall_peer(o) * 2 + core)
        return carry

    lax.fori_loop(0, S - 1, greet_span, 0)
    greet(me_s, partner)
    for copy in loads[1:]:
        copy.start()
    lax.fori_loop(0, K - 1, greet_wall, 0)

    def regroup(g, carry):
        for col in range(4):
            tmp[pl.ds(col * 64, 64), :] = forcing[g, col].astype(jnp.float32)
        for col in range(4):
            for y in range(4):
                piece = tmp[pl.ds(col * 64 + y, 16, stride=4), :].astype(jnp.bfloat16)
                send_f[col // 2, (col % 2) * 4 + y, lax.rem(g, F), g // F] = piece
        return carry

    loads[0].wait()
    lax.fori_loop(0, 2 * F, regroup, 0)

    pl.semaphore_wait(barrier, 2 * S - 1 + K - 1)

    def remote(src_ref, dst_ref, ss, rs, s, w):
        return pltpu.make_async_remote_copy(
            src_ref=src_ref, dst_ref=dst_ref, send_sem=ss, recv_sem=rs,
            device_id=(s, w), device_id_type=MESH,
        )

    def f_copy(ch, o):
        to = span_peer(o)
        return remote(send_f.at[ch, to], recv_f.at[ch, me_s], f_send.at[ch], f_recv.at[ch], to, me_w)

    def f_all(ch):
        some = pl.ds(0, S - 1)
        return remote(send_f.at[ch, some], recv_f.at[ch, some], f_send.at[ch], f_recv.at[ch], me_s, partner)

    def f_local(ch):
        return pltpu.make_async_copy(send_f.at[ch, me_s], recv_f.at[ch, me_s], loc.at[0, ch])

    def c_copy(n, ref, part):
        return remote(ref.at[:, pl.ds(other * 32, 32), :], part, c_send.at[n], c_recv.at[n], me_s, partner)

    c_copies = [c_copy(0, low_in, part_l), c_copy(1, upp_in, part_u), c_copy(2, piv_in, part_p)]

    def forcing_out(ch):
        f_local(ch).start()

        def start_f(o, carry):
            f_copy(ch, o).start()
            return carry

        lax.fori_loop(0, S - 1, start_f, 0)

    forcing_out(0)
    for copy in c_copies:
        copy.start()
    for copy in loads[1:]:
        copy.wait()

    def by_row(ref, first, dst, at):
        def step(g, carry):
            for j in range(F):
                tmp[pl.ds(j * 32, 32), :] = ref[g * F + j, pl.ds(first, 32), :].astype(jnp.float32)
            for j in range(F):
                for y in range(4):
                    dst[at * 4 + y, g // F, j, lax.rem(g, F)] = tmp[pl.ds(j * 32 + y, 8, stride=4), :]
            return carry

        lax.fori_loop(0, 2 * F, step, 0)

    mine = pl.multiple_of(core * 32, 32)
    by_row(low, mine, lf, core)
    by_row(upp, mine, uf, core)
    by_row(piv, mine, pf, core)
    dot = functools.partial(jnp.dot, precision=HI, preferred_element_type=jnp.float32)
    for f in range(F):
        line[0, f:f + 1, :] = factor[f, 0:1, :]
        line[1, f:f + 1, :] = factor[f, 1:2, :]
    factor_re = line[0, 0:F, :]
    factor_im = line[1, 0:F, :]
    first_re = (dot(factor_re, table[0]) + dot(factor_im, table[1])) * (1.0 / 128.0)
    first_im = (dot(factor_im, table[0]) - dot(factor_re, table[1])) * (1.0 / 128.0)
    line[0, 0:F, :] = first_re
    line[1, 0:F, :] = first_im

    def build(f, carry):
        turn = lambda row: pltpu.roll(jnp.broadcast_to(row, (128, 128)), 0, 1, stride=1, stride_axis=0)
        kr = turn(line[0, pl.ds(f, 1), :])
        ki = turn(line[1, pl.ds(f, 1), :])
        for rows, cols, block in ((0, 0, kr), (0, 128, -ki), (128, 0, ki), (128, 128, kr)):
            top = block.astype(jnp.bfloat16)
            a_hi[f, rows:rows + 128, cols:cols + 128] = top
            a_lo[f, rows:rows + 128, cols:cols + 128] = (block - top.astype(jnp.float32)).astype(jnp.bfloat16)
        return carry

    lax.fori_loop(0, F, build, 0)

    forcing_out(1)
    c_copies[0].wait()
    by_row(part_l, 0, lf, other)
    c_copies[1].wait()
    by_row(part_u, 0, uf, other)
    c_copies[2].wait()
    by_row(part_p, 0, pf, other)

    def forward_column(n, carry):
        v = (-lf[0, 0, n], -lf[0, 1, n])
        pre[0, 0, n] = v[0]
        pre[0, 1, n] = v[1]

        def step(y, v):
            w = apply(lf, y, [v])[0]
            w = (-w[0], -w[1])
            pre[y, 0, n] = w[0]
            pre[y, 1, n] = w[1]
            return w

        v = lax.fori_loop(1, ROWS, step, v)
        tm[0, 0, n] = v[0]
        tm[0, 1, n] = v[1]
        return carry

    lax.fori_loop(0, F, forward_column, 0)

    def r_copy(ch, to, c):
        return remote(
            send_r.at[ch, to * 2 + c], driv.at[ch, core * S + me_s], r_send.at[ch], r_recv.at[ch], to, chip * 2 + c
        )

    def r_all(ch):
        some = pl.ds(0, 2 * S - 1)
        return remote(send_r.at[ch, some], driv.at[ch, some], r_send.at[ch], r_recv.at[ch], me_s, partner)

    def r_local(ch):
        return pltpu.make_async_copy(send_r.at[ch, me_s * 2 + core], driv.at[ch, core * S + me_s], loc.at[2, ch])

    def filtered(ch, carry):
        f_local(ch).wait()
        f_all(ch).wait_recv()

        def field(f, carry):
            rhs = jnp.concatenate(
                [recv_f[ch, :, f, 0].reshape(128, 128), recv_f[ch, :, f, 1].reshape(128, 128)], axis=0
            )
            res = jnp.dot(a_hi[f], rhs, preferred_element_type=jnp.float32) + jnp.dot(
                a_lo[f], rhs, preferred_element_type=jnp.float32
            )
            re = res[:128].reshape(2 * S, 8, 128)
            im = res[128:].reshape(2 * S, 8, 128)
            top = jnp.max(jnp.maximum(jnp.abs(re), jnp.abs(im)), axis=1, keepdims=True)
            scale = jnp.maximum(top * 1.01, 1e-30).astype(jnp.bfloat16).astype(jnp.float32)
            scales[:, pl.ds(f, 1), :] = scale
            send_r[ch, :, f] = encode(re, scale).astype(jnp.bfloat16)
            send_r[ch, :, F + f] = encode(im, scale).astype(jnp.bfloat16)
            return carry

        lax.fori_loop(0, F, field, 0)
        send_r[ch, :, 2 * F] = scales[...].astype(jnp.bfloat16)
        r_local(ch).start()

        def start_r(o, carry):
            to = span_peer(o)
            r_copy(ch, to, core).start()
            r_copy(ch, to, other).start()
            return carry

        lax.fori_loop(0, S - 1, start_r, 0)
        r_copy(ch, me_s, other).start()
        return carry

    def backward_column(n, carry):
        last = ROWS - 1
        v = (-uf[last, 0, n], -uf[last, 1, n])
        b = (pre[last, 0, n], pre[last, 1, n])

        def step(t, state):
            y = last - 1 - t
            v, b = state
            x, z = apply(uf, y, [v, b])
            return ((-x[0], -x[1]), (pre[y, 0, n] - z[0], pre[y, 1, n] - z[1]))

        v, b = lax.fori_loop(0, last, step, (v, b))
        tm[1, 0, n] = v[0]
        tm[1, 1, n] = v[1]
        tm[2, 0, n] = b[0]
        tm[2, 1, n] = b[1]
        return carry

    lax.fori_loop(0, 2, backward_column, 0)
    filtered(0, 0)

    lax.fori_loop(2, F, backward_column, 0)

    def halves(p, q):
        axis = p.ndim - 1
        left = lax.broadcasted_iota(jnp.int32, p.shape, axis) < 64
        return (
            jnp.where(left, p, pltpu.roll(q, 64, axis)),
            jnp.where(left, pltpu.roll(p, 64, axis), q),
        )

    def pack_t(g, carry):
        at = (g // F) * 32 + lax.rem(g, F) * F
        d0, d1 = halves(tm[g // F, 0, lax.rem(g, F)], tm[g // F, 1, lax.rem(g, F)])
        for i in range(F):
            send_t[pl.ds(at + i, 8, stride=TR), :] = d0[i]
            send_t[pl.ds(8 * TR + at + i, 8, stride=TR), :] = d1[i]
        return carry

    lax.fori_loop(0, 3 * F, pack_t, 0)

    def code_transfers(n, carry):
        encode_blocks(send_t, code_t, 2 * n, 2, 3, 4, 25)
        return carry

    lax.fori_loop(0, K // 2, code_transfers, 0)

    def t_copy(o):
        to = wall_peer(o)
        return remote(code_t.at[to], got_t.at[chip], t_send.at[0], t_recv.at[0], me_s, to * 2 + core)

    def t_all():
        some = pl.ds(0, K - 1)
        return remote(code_t.at[some], got_t.at[some], t_send.at[0], t_recv.at[0], me_s, partner)

    t_local = pltpu.make_async_copy(code_t.at[chip], got_t.at[chip], loc.at[1, 0])
    t_local.start()

    def start_t(o, carry):
        t_copy(o).start()
        return carry

    lax.fori_loop(0, K - 1, start_t, 0)

    filtered(1, 0)

    def a_copy(ch, o):
        to = wall_peer(o)
        return remote(
            code_a.at[ch * K + to], got_a.at[ch * K + chip], a_send.at[ch], a_recv.at[ch], me_s, to * 2 + core
        )

    def a_all(ch):
        some = pl.ds(ch * K, K - 1)
        return remote(code_a.at[some], got_a.at[some], a_send.at[ch], a_recv.at[ch], me_s, partner)

    def a_local(ch):
        return pltpu.make_async_copy(code_a.at[ch * K + chip], got_a.at[ch * K + chip], loc.at[3, ch])

    zero = jnp.zeros((F, 8, 128), jnp.float32)

    def put(ref, y, state):
        for n in range(2):
            ref[y, n, 0] = state[n][0]
            ref[y, n, 1] = state[n][1]

    def get(ref, y):
        return [(ref[y, n, 0], ref[y, n, 1]) for n in range(2)]

    def local_solve(ch, carry):
        r_local(ch).wait()
        r_all(ch).wait_recv()

        def forward(y, state):
            base = (y // 4) * S + lax.rem(y, 4)
            drive = []
            for n in range(2):
                code = driv[ch, base + 4 * n].astype(jnp.float32)
                scale = jnp.stack([jnp.broadcast_to(code[2 * F, f:f + 1], (8, 128)) for f in range(F)])
                drive.append((decode(code[:F], scale), decode(code[F:2 * F], scale)))
            source = apply(pf, y, drive)
            put(src.at[ch], y, source)
            state = sub(source, apply(lf, y, state))
            put(sw, y, state)
            return state

        a = lax.fori_loop(0, ROWS, forward, [(zero, zero), (zero, zero)])

        def backward(t, state):
            y = ROWS - 2 - t
            return sub(get(sw, y), apply(uf, y, state))

        c = lax.fori_loop(0, ROWS - 1, backward, a)
        base = ch * (K * AR)
        for g, (p, q) in enumerate(((a[0][0], a[1][0]), (a[0][1], a[1][1]), (c[0][0], c[1][0]), (c[0][1], c[1][1]))):
            d0, d1 = halves(p, q)
            for i in range(F):
                send_a[pl.ds(base + g * F + i, 8, stride=AR), :] = d0[i]
                send_a[pl.ds(base + 8 * AR + g * F + i, 8, stride=AR), :] = d1[i]
        for n in range(2):
            encode_blocks(send_a, code_a, ch * K + 8 * n, 8, 1, 3, 20)
        a_local(ch).start()

        def start_a(o, carry):
            a_copy(ch, o).start()
            return carry

        lax.fori_loop(0, K - 1, start_a, 0)
        return carry

    lax.fori_loop(0, 2, local_solve, 0)

    t_local.wait()
    t_all().wait_recv()

    def plain_transfers(n, carry):
        decode_blocks(got_t, recv_t, 2 * n, 2, 3, 4)
        return carry

    lax.fori_loop(0, K // 2, plain_transfers, 0)

    def expand(k, carry):
        for g in range(3 * F):
            rows = recv_t[pl.ds(k * TR + (g // F) * 32 + (g % F) * F, F), :]
            left = lax.broadcasted_iota(jnp.int32, rows.shape, 1) < 64
            turned = pltpu.roll(rows, 64, 1)
            te[k, g // F, 0, g % F, 0:F, :] = jnp.where(left, rows, turned)
            te[k, g // F, 1, g % F, 0:F, :] = jnp.where(left, turned, rows)
        return carry

    lax.fori_loop(0, K, expand, 0)

    def small(k, m, state, start):
        re, im = start
        for j in range(F):
            tr = te[k, m, 0, j, 0:F, :]
            ti = te[k, m, 1, j, 0:F, :]
            xr = state[0][j:j + 1]
            xi = state[1][j:j + 1]
            re = re + (tr * xr - ti * xi)
            im = im + (tr * xi + ti * xr)
        return re, im

    def s_copy(ch, o):
        to = wall_peer(o)
        return remote(
            code_s.at[ch * K + to], got_s.at[ch * K + chip], s_send.at[ch], s_recv.at[ch], me_s, to * 2 + core
        )

    def s_all(ch):
        some = pl.ds(ch * K, K - 1)
        return remote(code_s.at[some], got_s.at[some], s_send.at[ch], s_recv.at[ch], me_s, partner)

    def s_local(ch):
        return pltpu.make_async_copy(code_s.at[ch * K + chip], got_s.at[ch * K + chip], loc.at[4, ch])

    flat = jnp.zeros((F, 128), jnp.float32)

    def owner_scan(ch, carry):
        a_local(ch).wait()
        a_all(ch).wait_recv()
        for n in range(2):
            decode_blocks(got_a, recv_a, ch * K + 8 * n, 8, 1, 3)

        def forward(k, state):
            base = (ch * K + k) * AR
            send_s[pl.ds(base, F), :] = state[0]
            send_s[pl.ds(base + F, F), :] = state[1]
            a = (recv_a[pl.ds(base, F), :], recv_a[pl.ds(base + F, F), :])
            c = (recv_a[pl.ds(base + 2 * F, F), :], recv_a[pl.ds(base + 3 * F, F), :])
            q = small(k, 2, state, c)
            qb[k, 0, 0:F, :] = q[0]
            qb[k, 1, 0:F, :] = q[1]
            return small(k, 0, state, a)

        lax.fori_loop(0, K, forward, (flat, flat))

        def backward(t, state):
            k = K - 1 - t
            base = (ch * K + k) * AR
            send_s[pl.ds(base + 2 * F, F), :] = state[0]
            send_s[pl.ds(base + 3 * F, F), :] = state[1]
            return small(k, 1, state, (qb[k, 0, 0:F, :], qb[k, 1, 0:F, :]))

        lax.fori_loop(0, K, backward, (flat, flat))
        for n in range(2):
            encode_blocks(send_s, code_s, ch * K + 8 * n, 8, 1, 3, 20)
        s_local(ch).start()

        def start_s(o, carry):
            s_copy(ch, o).start()
            return carry

        lax.fori_loop(0, K - 1, start_s, 0)
        return carry

    lax.fori_loop(0, 2, owner_scan, 0)

    def o_copy(ch):
        return remote(
            resp.at[other, ch], out.at[:, pl.ds(2 * ch, 2), pl.ds(core * 32, 32), :],
            o_send.at[ch], o_recv.at[ch], me_s, partner,
        )

    def o_wait(ch):
        return remote(
            resp.at[other, ch], out.at[:, pl.ds(2 * ch, 2), pl.ds(other * 32, 32), :],
            o_send.at[ch], o_recv.at[ch], me_s, partner,
        )

    def o_local(ch):
        return pltpu.make_async_copy(
            resp.at[core, ch], out.at[:, pl.ds(2 * ch, 2), pl.ds(core * 32, 32), :], loc.at[5, ch]
        )

    def final(ch, carry):
        s_local(ch).wait()
        s_all(ch).wait_recv()
        for n in range(2):
            decode_blocks(got_s, recv_s, ch * K + 8 * n, 8, 1, 3)
        base = ch * (K * AR)

        def entering(g):
            e0 = jnp.stack([recv_s[pl.ds(base + g * F + i, 8, stride=AR), :] for i in range(F)])
            e1 = jnp.stack([recv_s[pl.ds(base + 8 * AR + g * F + i, 8, stride=AR), :] for i in range(F)])
            return halves(e0, e1)

        def pair(g):
            re = entering(g)
            im = entering(g + 1)
            return [(re[0], im[0]), (re[1], im[1])]

        def forward(y, state):
            state = sub(get(src.at[ch], y), apply(lf, y, state))
            put(sw, y, state)
            return state

        lax.fori_loop(0, ROWS, forward, pair(0))

        def backward(t, state):
            y = ROWS - 1 - t
            state = sub(get(sw, y), apply(uf, y, state))
            for n in range(2):
                for ri in range(2):
                    for i in range(F):
                        resp.at[y // 4, ch, ri * F + i, n][pl.ds(lax.rem(y, 4), 8, stride=4), :] = state[n][ri][i]
            return state

        lax.fori_loop(0, ROWS, backward, pair(2))
        o_local(ch).start()
        o_copy(ch).start()
        return carry

    lax.fori_loop(0, 2, final, 0)

    for ch in range(2):
        o_local(ch).wait()
        o_wait(ch).wait_recv()
        o_copy(ch).wait_send()
        f_all(ch).wait_send()
        r_all(ch).wait_send()
        a_all(ch).wait_send()
        s_all(ch).wait_send()
    t_all().wait_send()


def tables():
    n = np.arange(128)
    angle = (n[:, None] * n[None, :] % 128) * (2.0 * math.pi / 128)
    return np.stack([np.cos(angle), np.sin(angle)]).astype(np.float32)


def local(forcing, span_factor, pivot_inverse, step_lower, step_upper):
    f32, bf16 = jnp.float32, jnp.bfloat16
    dma = pltpu.SemaphoreType.DMA
    vm = pltpu.VMEM
    flat = [x.reshape(50, 64, 128) for x in (pivot_inverse, step_lower, step_upper)]
    coef = vm((ROWS, 2, F, F, 8, 128), f32)
    rows = vm((ROWS, 2, 2, F, 8, 128), f32)
    scratch = [
        vm((2 * F, 4, 64, 128), bf16), vm((F, 2, 128), f32), vm((2, 128, 128), f32),
        vm((50, 64, 128), bf16), vm((50, 64, 128), bf16), vm((50, 64, 128), bf16),
        vm((256, 128), f32),
        vm((2, 8, 128), f32),
        vm((2 * S, 8, 128), f32),
        vm((2, S, F, 2, 16, 128), bf16),
        vm((2, S, F, 2, 16, 128), bf16),
        vm((50, 32, 128), bf16), vm((50, 32, 128), bf16), vm((50, 32, 128), bf16),
        coef, coef, coef, coef,
        vm((3, 2, F, F, 8, 128), f32),
        vm((F, 256, 256), bf16), vm((F, 256, 256), bf16),
        vm((2, 2 * S, 2 * F + 1, 8, 128), bf16),
        vm((2, 2 * S, 2 * F + 1, 8, 128), bf16),
        vm((K * TR, 128), f32), vm((K * TR, 128), f32),
        vm((K, 3, 2, F, 8, 128), f32),
        vm((2 * K * AR, 128), f32), vm((2 * K * AR, 128), f32),
        vm((2 * K * AR, 128), f32), vm((2 * K * AR, 128), f32),
        vm((K, 12, 8, 128), bf16), vm((K, 12, 8, 128), bf16),
        vm((2 * K, 3, 8, 128), bf16), vm((2 * K, 3, 8, 128), bf16),
        vm((2 * K, 3, 8, 128), bf16), vm((2 * K, 3, 8, 128), bf16),
        vm((2, ROWS, 2, 2, F, 8, 128), f32),
        rows,
        vm((K, 2, 8, 128), f32),
        vm((2, 2, 2 * F, 2, 32, 128), f32),
        dma((3,)), dma((3,)),
        dma((2,)), dma((2,)),
        dma((2,)), dma((2,)),
        dma((1,)), dma((1,)),
        dma((2,)), dma((2,)),
        dma((2,)), dma((2,)),
        dma((2,)), dma((2,)),
        dma((6, 2)),
        dma((6,)),
    ]
    out = pl.pallas_call(
        kernel,
        out_shape=jax.ShapeDtypeStruct((2 * F, 4, 64, 128), f32),
        in_specs=[pl.BlockSpec(memory_space=pltpu.HBM)] * 6,
        out_specs=pl.BlockSpec(memory_space=pl.ANY),
        scratch_shapes=scratch,
        compiler_params=pltpu.CompilerParams(
            collective_id=0, has_side_effects=True, vmem_limit_bytes=34 << 20
        ),
    )(
        *[
            pltpu.with_memory_space_constraint(x, pltpu.HBM)
            for x in (
                forcing.reshape(2 * F, 4, 64, 128),
                jnp.swapaxes(span_factor, 0, 1),
                jnp.asarray(tables()),
                *flat,
            )
        ]
    )
    return out.reshape(2, F, 4, 16, 4, 128)


def solution(mesh):
    placed = P(None, None, None, "span", "wall", None)
    return jax.shard_map(
        local,
        mesh=mesh,
        in_specs=(placed, P(), placed, placed, placed),
        out_specs=placed,
        check_vma=False,
    )
```

```python
import functools
import math

import jax
import jax.numpy as jnp
import numpy as np
from jax import lax
from jax.experimental import pallas as pl
from jax.experimental.pallas import tpu as pltpu
from jax.sharding import PartitionSpec as P

MESH = pl.DeviceIdType.MESH
F = 5
S = 8
K = 16
ROWS = 8
TR = 80
AR = 24
HI = lax.Precision.HIGHEST
LEVELS = 29900.0
SHIFT = 117.0


def encode(x, scale):
    y = x * (LEVELS / scale)
    n = jnp.floor(jnp.abs(y) + 0.5)
    e = jnp.floor(n * (1.0 / 128.0))
    v = (1.0 + (n - 128.0 * e) * (1.0 / 128.0)) * jnp.exp2(e - SHIFT)
    return jnp.where(y < 0.0, -v, v)


def decode(v, scale):
    a = jnp.abs(v)
    e = jnp.floor(jnp.log2(a) + 0.002)
    n = 128.0 * (e + (SHIFT - 1.0)) + 128.0 * (a * jnp.exp2(-e))
    return jnp.where(v < 0.0, -n, n) * (scale * (1.0 / LEVELS))


def encode_blocks(src, dst, first, count, parts, tiles, used):
    rows = parts * tiles * 8
    x = src[pl.ds(pl.multiple_of(first * rows, 8), count * rows), :].reshape(count * parts, tiles, 8, 128)
    place = lax.broadcasted_iota(jnp.int32, x.shape, 1) * 8 + lax.broadcasted_iota(jnp.int32, x.shape, 2)
    good = place < used
    x = jnp.where(good, x, 0.0)
    top = jnp.max(jnp.max(jnp.abs(x), axis=1, keepdims=True), axis=2, keepdims=True)
    scale = jnp.maximum(top * 1.01, 1e-30).astype(jnp.bfloat16).astype(jnp.float32)
    code = jnp.where(good, encode(x, scale), scale).astype(jnp.bfloat16)
    dst[pl.ds(first, count)] = code.reshape(count, parts * tiles, 8, 128)


def decode_blocks(src, dst, first, count, parts, tiles):
    rows = parts * tiles * 8
    code = src[pl.ds(first, count)].astype(jnp.float32).reshape(count * parts, tiles, 8, 128)
    x = decode(code, code[:, tiles - 1:, 7:, :])
    dst[pl.ds(pl.multiple_of(first * rows, 8), count * rows), :] = x.reshape(count * rows, 128)


def by_matrix(place, values):
    return jnp.where(place < 25, values[0], jnp.where(place < 50, values[1], values[2]))


def encode_transfers(src, dst, first, count):
    x = src[pl.ds(pl.multiple_of(first * TR, 8), count * TR), :].reshape(count, TR // 8, 8, 128)
    place = lax.broadcasted_iota(jnp.int32, x.shape, 1) * 8 + lax.broadcasted_iota(jnp.int32, x.shape, 2)
    size = jnp.abs(x)
    scales = []
    for m in range(3):
        own = jnp.where((place >= 25 * m) & (place < 25 * m + 25), size, 0.0)
        top = jnp.max(jnp.max(own, axis=1, keepdims=True), axis=2, keepdims=True)
        scales.append(jnp.maximum(top * 1.01, 1e-30).astype(jnp.bfloat16).astype(jnp.float32))
    good = place < 75
    code = encode(jnp.where(good, x, 0.0), by_matrix(place, scales))
    tail = jnp.where(place == 76, scales[1], jnp.where(place == 77, scales[2], scales[0]))
    dst[pl.ds(first, count)] = jnp.where(good, code, tail).astype(jnp.bfloat16)


def decode_transfers(src, dst, first, count):
    code = src[pl.ds(first, count)].astype(jnp.float32)
    place = lax.broadcasted_iota(jnp.int32, code.shape, 1) * 8 + lax.broadcasted_iota(jnp.int32, code.shape, 2)
    scale = by_matrix(place, [code[:, 9:, 3 + m:4 + m, :] for m in range(3)])
    dst[pl.ds(pl.multiple_of(first * TR, 8), count * TR), :] = decode(code, scale).reshape(count * TR, 128)


def apply(coef, y, vectors):
    out = [None] * len(vectors)
    for j in range(F):
        c = coef[y, 0, j]
        d = coef[y, 1, j]
        e = coef[y, 2, j]
        for n, (vr, vi) in enumerate(vectors):
            xr = vr[j]
            xi = vi[j]
            p = (c * (xr + xi)[None], d * xr[None], e * xi[None])
            out[n] = p if out[n] is None else tuple(a + b for a, b in zip(out[n], p))
    return [(p[0] - p[2], p[0] + p[1]) for p in out]


def sub(a, b):
    return [(x[0] - y[0], x[1] - y[1]) for x, y in zip(a, b)]


def kernel(
    forcing_in, factor_in, table_in, piv_in, low_in, upp_in, out,
    forcing, factor, table, piv, low, upp, tmp, line, scales, send_f, recv_f, part_p, part_l, part_u, pf, lf, uf, pre, tm, a_hi, a_lo,
    send_r, driv, send_t, recv_t, te, send_a, recv_a, send_s, recv_s,
    code_t, got_t, code_a, got_a, code_s, got_s, src, sw, qb, resp,
    c_send, c_recv, f_send, f_recv, r_send, r_recv, t_send, t_recv, a_send, a_recv, s_send, s_recv,
    o_send, o_recv, loc, load,
):
    me_s = lax.axis_index("span")
    me_w = lax.axis_index("wall")
    core = lax.rem(me_w, 2)
    chip = me_w // 2
    other = 1 - core
    partner = chip * 2 + other

    def ordered(i, n, first):
        step = (i + 1) // 2
        return lax.rem(n // 2 + n + jnp.where(lax.rem(i, 2) == first, step, -step), n)

    def span_peer(o):
        y = lax.rem(me_s // 4 + 1 - lax.rem(o, 2), 2)
        x = lax.rem(lax.rem(me_s, 4) + ordered(o // 2, 4, 0), 4)
        return y * 4 + x

    def wall_peer(o):
        y = lax.rem(chip // 8 + 1 - o // 8, 2)
        z = lax.rem(lax.rem(chip, 8) + ordered(lax.rem(o, 8), 8, 1), 8)
        return y * 8 + z

    loads = [
        pltpu.make_async_copy(a, b, load.at[n])
        for n, (a, b) in enumerate(
            (
                (forcing_in, forcing), (low_in, low), (upp_in, upp), (piv_in, piv),
                (factor_in, factor), (table_in, table),
            )
        )
    ]
    loads[0].start()

    barrier = pltpu.get_barrier_semaphore()

    def greet(s, w):
        pl.semaphore_signal(barrier, inc=1, device_id=(s, w), device_id_type=MESH)

    def greet_span(o, carry):
        greet(span_peer(o), me_w)
        greet(span_peer(o), partner)
        return carry

    def greet_wall(o, carry):
        greet(me_s, wall_peer(o) * 2 + core)
        return carry

    lax.fori_loop(0, S - 1, greet_span, 0)
    greet(me_s, partner)
    for copy in loads[1:]:
        copy.start()
    lax.fori_loop(0, K - 1, greet_wall, 0)

    def regroup(ch):
        def step(g, carry):
            for n in range(2):
                tmp[pl.ds(n * 64, 64), :] = forcing[g, 2 * ch + n].astype(jnp.float32)
            for n in range(2):
                for y in range(4):
                    piece = tmp[pl.ds(n * 64 + y, 16, stride=4), :].astype(jnp.bfloat16)
                    send_f[ch, n * 4 + y, lax.rem(g, F), g // F] = piece
            return carry

        lax.fori_loop(0, 2 * F, step, 0)

    loads[0].wait()
    regroup(0)

    pl.semaphore_wait(barrier, 2 * S - 1 + K - 1)

    def remote(src_ref, dst_ref, ss, rs, s, w):
        return pltpu.make_async_remote_copy(
            src_ref=src_ref, dst_ref=dst_ref, send_sem=ss, recv_sem=rs,
            device_id=(s, w), device_id_type=MESH,
        )

    def f_copy(ch, o):
        to = span_peer(o)
        return remote(send_f.at[ch, to], recv_f.at[ch, me_s], f_send.at[ch], f_recv.at[ch], to, me_w)

    def f_all(ch):
        some = pl.ds(0, S - 1)
        return remote(send_f.at[ch, some], recv_f.at[ch, some], f_send.at[ch], f_recv.at[ch], me_s, partner)

    def f_local(ch):
        return pltpu.make_async_copy(send_f.at[ch, me_s], recv_f.at[ch, me_s], loc.at[0, ch])

    def c_copy(n, ref, part):
        return remote(ref.at[:, pl.ds(other * 32, 32), :], part, c_send.at[n], c_recv.at[n], me_s, partner)

    c_copies = [c_copy(0, low_in, part_l), c_copy(1, upp_in, part_u), c_copy(2, piv_in, part_p)]

    def forcing_out(ch):
        f_local(ch).start()

        def start_f(o, carry):
            f_copy(ch, o).start()
            return carry

        lax.fori_loop(0, S - 1, start_f, 0)

    forcing_out(0)
    for copy in c_copies:
        copy.start()
    regroup(1)
    for copy in loads[1:]:
        copy.wait()

    def by_row(ref, first, dst, at):
        def step(i, carry):
            for ri in range(2):
                for j in range(F):
                    tmp[pl.ds((ri * F + j) * 32, 32), :] = ref[(ri * F + i) * F + j, pl.ds(first, 32), :].astype(jnp.float32)
            for j in range(F):
                for y in range(4):
                    re = tmp[pl.ds(j * 32 + y, 8, stride=4), :]
                    im = tmp[pl.ds((F + j) * 32 + y, 8, stride=4), :]
                    dst[at * 4 + y, 0, j, i] = re
                    dst[at * 4 + y, 1, j, i] = im - re
                    dst[at * 4 + y, 2, j, i] = im + re
            return carry

        lax.fori_loop(0, F, step, 0)

    mine = pl.multiple_of(core * 32, 32)
    by_row(low, mine, lf, core)
    by_row(upp, mine, uf, core)
    dot = functools.partial(jnp.dot, precision=HI, preferred_element_type=jnp.float32)
    for f in range(F):
        line[0, f:f + 1, :] = factor[f, 0:1, :]
        line[1, f:f + 1, :] = factor[f, 1:2, :]
    factor_re = line[0, 0:F, :]
    factor_im = line[1, 0:F, :]
    first_re = (dot(factor_re, table[0]) + dot(factor_im, table[1])) * (1.0 / 128.0)
    first_im = (dot(factor_im, table[0]) - dot(factor_re, table[1])) * (1.0 / 128.0)
    line[0, 0:F, :] = first_re
    line[1, 0:F, :] = first_im

    def build(f, carry):
        turn = lambda row: pltpu.roll(jnp.broadcast_to(row, (128, 128)), 0, 1, stride=1, stride_axis=0)
        kr = turn(line[0, pl.ds(f, 1), :])
        ki = turn(line[1, pl.ds(f, 1), :])
        for rows, cols, block in ((0, 0, kr), (0, 128, -ki), (128, 0, ki), (128, 128, kr)):
            top = block.astype(jnp.bfloat16)
            a_hi[f, rows:rows + 128, cols:cols + 128] = top
            a_lo[f, rows:rows + 128, cols:cols + 128] = (block - top.astype(jnp.float32)).astype(jnp.bfloat16)
        return carry

    lax.fori_loop(0, F, build, 0)

    forcing_out(1)
    c_copies[0].wait()
    by_row(part_l, 0, lf, other)
    c_copies[1].wait()
    by_row(part_u, 0, uf, other)

    def forward_columns(columns):
        state = [(-lf[0, 0, n], -(lf[0, 0, n] + lf[0, 1, n])) for n in columns]
        for n, v in zip(columns, state):
            pre[0, 0, n] = v[0]
            pre[0, 1, n] = v[1]

        def step(y, state):
            state = [(-w[0], -w[1]) for w in apply(lf, y, state)]
            for n, v in zip(columns, state):
                pre[y, 0, n] = v[0]
                pre[y, 1, n] = v[1]
            return state

        for n, v in zip(columns, lax.fori_loop(1, ROWS, step, state)):
            tm[0, 0, n] = v[0]
            tm[0, 1, n] = v[1]

    def forward_pair(p, carry):
        forward_columns([2 * p, 2 * p + 1])
        return carry

    lax.fori_loop(0, 2, forward_pair, 0)
    forward_columns([4])

    def r_copy(ch, to, c):
        return remote(
            send_r.at[ch, to * 2 + c], driv.at[ch, core * S + me_s], r_send.at[ch], r_recv.at[ch], to, chip * 2 + c
        )

    def r_all(ch):
        some = pl.ds(0, 2 * S - 1)
        return remote(send_r.at[ch, some], driv.at[ch, some], r_send.at[ch], r_recv.at[ch], me_s, partner)

    def r_local(ch):
        return pltpu.make_async_copy(send_r.at[ch, me_s * 2 + core], driv.at[ch, core * S + me_s], loc.at[2, ch])

    def filtered(ch, carry):
        f_local(ch).wait()
        f_all(ch).wait_recv()

        def field(f, carry):
            rhs = jnp.concatenate(
                [recv_f[ch, :, f, 0].reshape(128, 128), recv_f[ch, :, f, 1].reshape(128, 128)], axis=0
            )
            res = jnp.dot(a_hi[f], rhs, preferred_element_type=jnp.float32) + jnp.dot(
                a_lo[f], rhs, preferred_element_type=jnp.float32
            )
            re = res[:128].reshape(2 * S, 8, 128)
            im = res[128:].reshape(2 * S, 8, 128)
            top = jnp.max(jnp.maximum(jnp.abs(re), jnp.abs(im)), axis=1, keepdims=True)
            scale = jnp.maximum(top * 1.01, 1e-30).astype(jnp.bfloat16).astype(jnp.float32)
            scales[:, pl.ds(f, 1), :] = scale
            send_r[ch, :, f] = encode(re, scale).astype(jnp.bfloat16)
            send_r[ch, :, F + f] = encode(im, scale).astype(jnp.bfloat16)
            return carry

        lax.fori_loop(0, F, field, 0)
        send_r[ch, :, 2 * F] = scales[...].astype(jnp.bfloat16)
        r_local(ch).start()

        def start_r(o, carry):
            to = span_peer(o)
            r_copy(ch, to, core).start()
            r_copy(ch, to, other).start()
            return carry

        lax.fori_loop(0, S - 1, start_r, 0)
        r_copy(ch, me_s, other).start()
        return carry

    def backward_column(n, carry):
        last = ROWS - 1
        v = (-uf[last, 0, n], -(uf[last, 0, n] + uf[last, 1, n]))
        b = (pre[last, 0, n], pre[last, 1, n])

        def step(t, state):
            y = last - 1 - t
            v, b = state
            x, z = apply(uf, y, [v, b])
            return ((-x[0], -x[1]), (pre[y, 0, n] - z[0], pre[y, 1, n] - z[1]))

        v, b = lax.fori_loop(0, last, step, (v, b))
        tm[1, 0, n] = v[0]
        tm[1, 1, n] = v[1]
        tm[2, 0, n] = b[0]
        tm[2, 1, n] = b[1]
        return carry


    lax.fori_loop(0, 3, backward_column, 0)
    filtered(0, 0)
    filtered(1, 0)
    lax.fori_loop(3, F, backward_column, 0)

    def halves(p, q):
        axis = p.ndim - 1
        left = lax.broadcasted_iota(jnp.int32, p.shape, axis) < 64
        return (
            jnp.where(left, p, pltpu.roll(q, 64, axis)),
            jnp.where(left, pltpu.roll(p, 64, axis), q),
        )

    def pack_t(g, carry):
        at = g * F
        d0, d1 = halves(tm[g // F, 0, lax.rem(g, F)], tm[g // F, 1, lax.rem(g, F)])
        for i in range(F):
            send_t[pl.ds(at + i, 8, stride=TR), :] = d0[i]
            send_t[pl.ds(8 * TR + at + i, 8, stride=TR), :] = d1[i]
        return carry

    lax.fori_loop(0, 3 * F, pack_t, 0)

    def code_transfers(n, carry):
        encode_transfers(send_t, code_t, 2 * n, 2)
        return carry

    lax.fori_loop(0, K // 2, code_transfers, 0)

    def t_copy(o):
        to = wall_peer(o)
        return remote(code_t.at[to], got_t.at[chip], t_send.at[0], t_recv.at[0], me_s, to * 2 + core)

    def t_all():
        some = pl.ds(0, K - 1)
        return remote(code_t.at[some], got_t.at[some], t_send.at[0], t_recv.at[0], me_s, partner)

    t_local = pltpu.make_async_copy(code_t.at[chip], got_t.at[chip], loc.at[1, 0])
    t_local.start()

    def start_t(o, carry):
        t_copy(o).start()
        return carry

    lax.fori_loop(0, K - 1, start_t, 0)

    by_row(piv, mine, pf, core)
    c_copies[2].wait()
    by_row(part_p, 0, pf, other)

    def a_copy(ch, o):
        to = wall_peer(o)
        return remote(
            code_a.at[ch * K + to], got_a.at[ch * K + chip], a_send.at[ch], a_recv.at[ch], me_s, to * 2 + core
        )

    def a_all(ch):
        some = pl.ds(ch * K, K - 1)
        return remote(code_a.at[some], got_a.at[some], a_send.at[ch], a_recv.at[ch], me_s, partner)

    def a_local(ch):
        return pltpu.make_async_copy(code_a.at[ch * K + chip], got_a.at[ch * K + chip], loc.at[3, ch])

    zero = jnp.zeros((F, 8, 128), jnp.float32)

    def put(ref, y, state):
        for n in range(2):
            ref[y, n, 0] = state[n][0]
            ref[y, n, 1] = state[n][1]

    def get(ref, y):
        return [(ref[y, n, 0], ref[y, n, 1]) for n in range(2)]

    def local_solve(ch, carry):
        r_local(ch).wait()
        r_all(ch).wait_recv()

        def forward(y, state):
            base = (y // 4) * S + lax.rem(y, 4)
            drive = []
            for n in range(2):
                code = driv[ch, base + 4 * n].astype(jnp.float32)
                scale = jnp.stack([jnp.broadcast_to(code[2 * F, f:f + 1], (8, 128)) for f in range(F)])
                drive.append((decode(code[:F], scale), decode(code[F:2 * F], scale)))
            source = apply(pf, y, drive)
            put(src.at[ch], y, source)
            state = sub(source, apply(lf, y, state))
            put(sw, y, state)
            return state

        a = lax.fori_loop(0, ROWS, forward, [(zero, zero), (zero, zero)])

        def backward(t, state):
            y = ROWS - 2 - t
            return sub(get(sw, y), apply(uf, y, state))

        c = lax.fori_loop(0, ROWS - 1, backward, a)
        base = ch * (K * AR)
        for g, (p, q) in enumerate(((a[0][0], a[1][0]), (a[0][1], a[1][1]), (c[0][0], c[1][0]), (c[0][1], c[1][1]))):
            d0, d1 = halves(p, q)
            for i in range(F):
                send_a[pl.ds(base + g * F + i, 8, stride=AR), :] = d0[i]
                send_a[pl.ds(base + 8 * AR + g * F + i, 8, stride=AR), :] = d1[i]
        for n in range(2):
            encode_blocks(send_a, code_a, ch * K + 8 * n, 8, 1, 3, 20)
        a_local(ch).start()

        def start_a(o, carry):
            a_copy(ch, o).start()
            return carry

        lax.fori_loop(0, K - 1, start_a, 0)
        return carry

    local_solve(0, 0)

    local_solve(1, 0)

    t_local.wait()
    t_all().wait_recv()

    def plain_transfers(n, carry):
        decode_transfers(got_t, recv_t, 2 * n, 2)
        return carry

    lax.fori_loop(0, K // 2, plain_transfers, 0)

    def expand(k, carry):
        for g in range(3 * F):
            rows = recv_t[pl.ds(k * TR + g * F, F), :]
            left = lax.broadcasted_iota(jnp.int32, rows.shape, 1) < 64
            turned = pltpu.roll(rows, 64, 1)
            te[k, g // F, 0, g % F, 0:F, :] = jnp.where(left, rows, turned)
            te[k, g // F, 1, g % F, 0:F, :] = jnp.where(left, turned, rows)
        return carry

    lax.fori_loop(0, K, expand, 0)

    def small(k, m, state, start):
        re, im = start
        for j in range(F):
            tr = te[k, m, 0, j, 0:F, :]
            ti = te[k, m, 1, j, 0:F, :]
            xr = state[0][j:j + 1]
            xi = state[1][j:j + 1]
            re = re + (tr * xr - ti * xi)
            im = im + (tr * xi + ti * xr)
        return re, im

    def s_copy(ch, o):
        to = wall_peer(o)
        return remote(
            code_s.at[ch * K + to], got_s.at[ch * K + chip], s_send.at[ch], s_recv.at[ch], me_s, to * 2 + core
        )

    def s_all(ch):
        some = pl.ds(ch * K, K - 1)
        return remote(code_s.at[some], got_s.at[some], s_send.at[ch], s_recv.at[ch], me_s, partner)

    def s_local(ch):
        return pltpu.make_async_copy(code_s.at[ch * K + chip], got_s.at[ch * K + chip], loc.at[4, ch])

    flat = jnp.zeros((F, 128), jnp.float32)

    def owner_scan(ch, carry):
        a_local(ch).wait()
        a_all(ch).wait_recv()
        for n in range(2):
            decode_blocks(got_a, recv_a, ch * K + 8 * n, 8, 1, 3)

        def forward(k, state):
            base = (ch * K + k) * AR
            send_s[pl.ds(base, F), :] = state[0]
            send_s[pl.ds(base + F, F), :] = state[1]
            a = (recv_a[pl.ds(base, F), :], recv_a[pl.ds(base + F, F), :])
            c = (recv_a[pl.ds(base + 2 * F, F), :], recv_a[pl.ds(base + 3 * F, F), :])
            q = small(k, 2, state, c)
            qb[k, 0, 0:F, :] = q[0]
            qb[k, 1, 0:F, :] = q[1]
            return small(k, 0, state, a)

        lax.fori_loop(0, K, forward, (flat, flat))

        def backward(t, state):
            k = K - 1 - t
            base = (ch * K + k) * AR
            send_s[pl.ds(base + 2 * F, F), :] = state[0]
            send_s[pl.ds(base + 3 * F, F), :] = state[1]
            return small(k, 1, state, (qb[k, 0, 0:F, :], qb[k, 1, 0:F, :]))

        lax.fori_loop(0, K, backward, (flat, flat))
        for n in range(2):
            encode_blocks(send_s, code_s, ch * K + 8 * n, 8, 1, 3, 20)
        s_local(ch).start()

        def start_s(o, carry):
            s_copy(ch, o).start()
            return carry

        lax.fori_loop(0, K - 1, start_s, 0)
        return carry

    lax.fori_loop(0, 2, owner_scan, 0)

    def o_copy(ch):
        return remote(
            resp.at[other, ch], out.at[:, pl.ds(2 * ch, 2), pl.ds(core * 32, 32), :],
            o_send.at[ch], o_recv.at[ch], me_s, partner,
        )

    def o_wait(ch):
        return remote(
            resp.at[other, ch], out.at[:, pl.ds(2 * ch, 2), pl.ds(other * 32, 32), :],
            o_send.at[ch], o_recv.at[ch], me_s, partner,
        )

    def o_local(ch):
        return pltpu.make_async_copy(
            resp.at[core, ch], out.at[:, pl.ds(2 * ch, 2), pl.ds(core * 32, 32), :], loc.at[5, ch]
        )

    def final(ch, carry):
        s_local(ch).wait()
        s_all(ch).wait_recv()
        for n in range(2):
            decode_blocks(got_s, recv_s, ch * K + 8 * n, 8, 1, 3)
        base = ch * (K * AR)

        def entering(g):
            e0 = jnp.stack([recv_s[pl.ds(base + g * F + i, 8, stride=AR), :] for i in range(F)])
            e1 = jnp.stack([recv_s[pl.ds(base + 8 * AR + g * F + i, 8, stride=AR), :] for i in range(F)])
            return halves(e0, e1)

        def pair(g):
            re = entering(g)
            im = entering(g + 1)
            return [(re[0], im[0]), (re[1], im[1])]

        def forward(y, state):
            state = sub(get(src.at[ch], y), apply(lf, y, state))
            put(sw, y, state)
            return state

        lax.fori_loop(0, ROWS, forward, pair(0))

        def backward(t, state):
            y = ROWS - 1 - t
            state = sub(get(sw, y), apply(uf, y, state))
            for n in range(2):
                for ri in range(2):
                    for i in range(F):
                        resp.at[y // 4, ch, ri * F + i, n][pl.ds(lax.rem(y, 4), 8, stride=4), :] = state[n][ri][i]
            return state

        lax.fori_loop(0, ROWS, backward, pair(2))
        o_local(ch).start()
        o_copy(ch).start()
        return carry

    lax.fori_loop(0, 2, final, 0)

    for ch in range(2):
        o_local(ch).wait()
        o_wait(ch).wait_recv()
        o_copy(ch).wait_send()
        f_all(ch).wait_send()
        r_all(ch).wait_send()
        a_all(ch).wait_send()
        s_all(ch).wait_send()
    t_all().wait_send()


def tables():
    n = np.arange(128)
    angle = (n[:, None] * n[None, :] % 128) * (2.0 * math.pi / 128)
    return np.stack([np.cos(angle), np.sin(angle)]).astype(np.float32)


def local(forcing, span_factor, pivot_inverse, step_lower, step_upper):
    f32, bf16 = jnp.float32, jnp.bfloat16
    dma = pltpu.SemaphoreType.DMA
    vm = pltpu.VMEM
    flat = [x.reshape(50, 64, 128) for x in (pivot_inverse, step_lower, step_upper)]
    coef = vm((ROWS, 3, F, F, 8, 128), f32)
    rows = vm((ROWS, 2, 2, F, 8, 128), f32)
    scratch = [
        vm((2 * F, 4, 64, 128), bf16), vm((F, 2, 128), f32), vm((2, 128, 128), f32),
        vm((50, 64, 128), bf16), vm((50, 64, 128), bf16), vm((50, 64, 128), bf16),
        vm((2 * F * 32, 128), f32),
        vm((2, 8, 128), f32),
        vm((2 * S, 8, 128), f32),
        vm((2, S, F, 2, 16, 128), bf16),
        vm((2, S, F, 2, 16, 128), bf16),
        vm((50, 32, 128), bf16), vm((50, 32, 128), bf16), vm((50, 32, 128), bf16),
        coef, coef, coef, vm((ROWS, 2, F, F, 8, 128), f32),
        vm((3, 2, F, F, 8, 128), f32),
        vm((F, 256, 256), bf16), vm((F, 256, 256), bf16),
        vm((2, 2 * S, 2 * F + 1, 8, 128), bf16),
        vm((2, 2 * S, 2 * F + 1, 8, 128), bf16),
        vm((K * TR, 128), f32), vm((K * TR, 128), f32),
        vm((K, 3, 2, F, 8, 128), f32),
        vm((2 * K * AR, 128), f32), vm((2 * K * AR, 128), f32),
        vm((2 * K * AR, 128), f32), vm((2 * K * AR, 128), f32),
        vm((K, TR // 8, 8, 128), bf16), vm((K, TR // 8, 8, 128), bf16),
        vm((2 * K, 3, 8, 128), bf16), vm((2 * K, 3, 8, 128), bf16),
        vm((2 * K, 3, 8, 128), bf16), vm((2 * K, 3, 8, 128), bf16),
        vm((2, ROWS, 2, 2, F, 8, 128), f32),
        rows,
        vm((K, 2, 8, 128), f32),
        vm((2, 2, 2 * F, 2, 32, 128), f32),
        dma((3,)), dma((3,)),
        dma((2,)), dma((2,)),
        dma((2,)), dma((2,)),
        dma((1,)), dma((1,)),
        dma((2,)), dma((2,)),
        dma((2,)), dma((2,)),
        dma((2,)), dma((2,)),
        dma((6, 2)),
        dma((6,)),
    ]
    out = pl.pallas_call(
        kernel,
        out_shape=jax.ShapeDtypeStruct((2 * F, 4, 64, 128), f32),
        in_specs=[pl.BlockSpec(memory_space=pltpu.HBM)] * 6,
        out_specs=pl.BlockSpec(memory_space=pl.ANY),
        scratch_shapes=scratch,
        compiler_params=pltpu.CompilerParams(
            collective_id=0, has_side_effects=True, vmem_limit_bytes=34 << 20
        ),
    )(
        *[
            pltpu.with_memory_space_constraint(x, pltpu.HBM)
            for x in (
                forcing.reshape(2 * F, 4, 64, 128),
                jnp.swapaxes(span_factor, 0, 1),
                jnp.asarray(tables()),
                *flat,
            )
        ]
    )
    return out.reshape(2, F, 4, 16, 4, 128)


def solution(mesh):
    placed = P(None, None, None, "span", "wall", None)
    return jax.shard_map(
        local,
        mesh=mesh,
        in_specs=(placed, P(), placed, placed, placed),
        out_specs=placed,
        check_vma=False,
    )
```

```python
import functools
import math

import jax
import jax.numpy as jnp
import numpy as np
from jax import lax
from jax.experimental import pallas as pl
from jax.experimental.pallas import tpu as pltpu
from jax.sharding import PartitionSpec as P

MESH = pl.DeviceIdType.MESH
F = 5
S = 8
K = 16
ROWS = 8
TR = 80
AR = 24
HI = lax.Precision.HIGHEST
LEVELS = 29900.0
SHIFT = 117.0


def encode(x, scale):
    y = x * (LEVELS / scale)
    n = jnp.floor(jnp.abs(y) + 0.5)
    e = jnp.floor(n * (1.0 / 128.0))
    v = (1.0 + (n - 128.0 * e) * (1.0 / 128.0)) * jnp.exp2(e - SHIFT)
    return jnp.where(y < 0.0, -v, v)


def decode(v, scale):
    a = jnp.abs(v)
    e = jnp.floor(jnp.log2(a) + 0.002)
    n = 128.0 * (e + (SHIFT - 1.0)) + 128.0 * (a * jnp.exp2(-e))
    return jnp.where(v < 0.0, -n, n) * (scale * (1.0 / LEVELS))


def encode_blocks(src, dst, first, count, parts, tiles, used):
    rows = parts * tiles * 8
    x = src[pl.ds(pl.multiple_of(first * rows, 8), count * rows), :].reshape(count * parts, tiles, 8, 128)
    place = lax.broadcasted_iota(jnp.int32, x.shape, 1) * 8 + lax.broadcasted_iota(jnp.int32, x.shape, 2)
    good = place < used
    x = jnp.where(good, x, 0.0)
    top = jnp.max(jnp.max(jnp.abs(x), axis=1, keepdims=True), axis=2, keepdims=True)
    scale = jnp.maximum(top * 1.01, 1e-30).astype(jnp.bfloat16).astype(jnp.float32)
    code = jnp.where(good, encode(x, scale), scale).astype(jnp.bfloat16)
    dst[pl.ds(first, count)] = code.reshape(count, parts * tiles, 8, 128)


def decode_blocks(src, dst, first, count, parts, tiles):
    rows = parts * tiles * 8
    code = src[pl.ds(first, count)].astype(jnp.float32).reshape(count * parts, tiles, 8, 128)
    x = decode(code, code[:, tiles - 1:, 7:, :])
    dst[pl.ds(pl.multiple_of(first * rows, 8), count * rows), :] = x.reshape(count * rows, 128)


def by_matrix(place, values):
    return jnp.where(place < 25, values[0], jnp.where(place < 50, values[1], values[2]))


def encode_transfers(src, dst, first, count):
    x = src[pl.ds(pl.multiple_of(first * TR, 8), count * TR), :].reshape(count, TR // 8, 8, 128)
    place = lax.broadcasted_iota(jnp.int32, x.shape, 1) * 8 + lax.broadcasted_iota(jnp.int32, x.shape, 2)
    size = jnp.abs(x)
    scales = []
    for m in range(3):
        own = jnp.where((place >= 25 * m) & (place < 25 * m + 25), size, 0.0)
        top = jnp.max(jnp.max(own, axis=1, keepdims=True), axis=2, keepdims=True)
        scales.append(jnp.maximum(top * 1.01, 1e-30).astype(jnp.bfloat16).astype(jnp.float32))
    good = place < 75
    code = encode(jnp.where(good, x, 0.0), by_matrix(place, scales))
    tail = jnp.where(place == 76, scales[1], jnp.where(place == 77, scales[2], scales[0]))
    dst[pl.ds(first, count)] = jnp.where(good, code, tail).astype(jnp.bfloat16)


def decode_transfers(src, dst, first, count):
    code = src[pl.ds(first, count)].astype(jnp.float32)
    place = lax.broadcasted_iota(jnp.int32, code.shape, 1) * 8 + lax.broadcasted_iota(jnp.int32, code.shape, 2)
    scale = by_matrix(place, [code[:, 9:, 3 + m:4 + m, :] for m in range(3)])
    dst[pl.ds(pl.multiple_of(first * TR, 8), count * TR), :] = decode(code, scale).reshape(count * TR, 128)


def apply(coef, y, vectors):
    out = [None] * len(vectors)
    for j in range(F):
        c = coef[y, 0, j]
        d = coef[y, 1, j]
        e = coef[y, 2, j]
        for n, (vr, vi) in enumerate(vectors):
            xr = vr[j]
            xi = vi[j]
            p = (c * (xr + xi)[None], d * xr[None], e * xi[None])
            out[n] = p if out[n] is None else tuple(a + b for a, b in zip(out[n], p))
    return [(p[0] - p[2], p[0] + p[1]) for p in out]


def sub(a, b):
    return [(x[0] - y[0], x[1] - y[1]) for x, y in zip(a, b)]


def kernel(
    forcing_in, factor_in, table_in, piv_in, low_in, upp_in, out,
    forcing, factor, table, piv, low, upp, tmp, line, scales, send_f, recv_f, part_p, part_l, part_u, pf, lf, uf, pre, tm, a_hi, a_lo,
    send_r, driv, send_t, recv_t, te, send_a, recv_a, send_s, recv_s,
    code_t, got_t, code_a, got_a, code_s, got_s, src, sw, qb, resp,
    c_send, c_recv, f_send, f_recv, r_send, r_recv, t_send, t_recv, a_send, a_recv, s_send, s_recv,
    o_send, o_recv, loc, load,
):
    me_s = lax.axis_index("span")
    me_w = lax.axis_index("wall")
    core = lax.rem(me_w, 2)
    chip = me_w // 2
    other = 1 - core
    partner = chip * 2 + other

    def ordered(i, n, first):
        step = (i + 1) // 2
        return lax.rem(n // 2 + n + jnp.where(lax.rem(i, 2) == first, step, -step), n)

    def span_peer(o):
        y = lax.rem(me_s // 4 + 1 - lax.rem(o, 2), 2)
        x = lax.rem(lax.rem(me_s, 4) + ordered(o // 2, 4, 0), 4)
        return y * 4 + x

    def wall_peer(o):
        y = lax.rem(chip // 8 + 1 - o // 8, 2)
        z = lax.rem(lax.rem(chip, 8) + ordered(lax.rem(o, 8), 8, 1), 8)
        return y * 8 + z

    loads = [
        pltpu.make_async_copy(a, b, load.at[n])
        for n, (a, b) in enumerate(
            (
                (forcing_in, forcing), (low_in, low), (upp_in, upp), (piv_in, piv),
                (factor_in, factor), (table_in, table),
            )
        )
    ]
    loads[0].start()

    barrier = pltpu.get_barrier_semaphore()

    def greet(s, w):
        pl.semaphore_signal(barrier, inc=1, device_id=(s, w), device_id_type=MESH)

    def greet_span(o, carry):
        greet(span_peer(o), me_w)
        greet(span_peer(o), partner)
        return carry

    def greet_wall(o, carry):
        greet(me_s, wall_peer(o) * 2 + core)
        return carry

    lax.fori_loop(0, S - 1, greet_span, 0)
    greet(me_s, partner)
    for copy in loads[1:]:
        copy.start()
    lax.fori_loop(0, K - 1, greet_wall, 0)

    def regroup(ch):
        def step(g, carry):
            for n in range(2):
                tmp[pl.ds(n * 64, 64), :] = forcing[g, 2 * ch + n].astype(jnp.float32)
            for n in range(2):
                for y in range(4):
                    piece = tmp[pl.ds(n * 64 + y, 16, stride=4), :].astype(jnp.bfloat16)
                    send_f[ch, n * 4 + y, lax.rem(g, F), g // F] = piece
            return carry

        lax.fori_loop(0, 2 * F, step, 0)

    loads[0].wait()
    regroup(0)

    pl.semaphore_wait(barrier, 2 * S - 1 + K - 1)

    def remote(src_ref, dst_ref, ss, rs, s, w):
        return pltpu.make_async_remote_copy(
            src_ref=src_ref, dst_ref=dst_ref, send_sem=ss, recv_sem=rs,
            device_id=(s, w), device_id_type=MESH,
        )

    def f_copy(ch, o):
        to = span_peer(o)
        return remote(send_f.at[ch, to], recv_f.at[ch, me_s], f_send.at[ch], f_recv.at[ch], to, me_w)

    def f_all(ch):
        some = pl.ds(0, S - 1)
        return remote(send_f.at[ch, some], recv_f.at[ch, some], f_send.at[ch], f_recv.at[ch], me_s, partner)

    def f_local(ch):
        return pltpu.make_async_copy(send_f.at[ch, me_s], recv_f.at[ch, me_s], loc.at[0, ch])

    def c_copy(n, ref, part):
        return remote(ref.at[:, pl.ds(other * 32, 32), :], part, c_send.at[n], c_recv.at[n], me_s, partner)

    c_copies = [c_copy(0, low_in, part_l), c_copy(1, upp_in, part_u), c_copy(2, piv_in, part_p)]

    def forcing_out(ch):
        f_local(ch).start()

        def start_f(o, carry):
            f_copy(ch, o).start()
            return carry

        lax.fori_loop(0, S - 1, start_f, 0)

    forcing_out(0)
    for copy in c_copies:
        copy.start()
    regroup(1)
    for copy in loads[1:]:
        copy.wait()

    def by_row(ref, first, dst, at):
        def step(i, carry):
            for ri in range(2):
                for j in range(F):
                    tmp[pl.ds((ri * F + j) * 32, 32), :] = ref[(ri * F + i) * F + j, pl.ds(first, 32), :].astype(jnp.float32)
            for j in range(F):
                for y in range(4):
                    re = tmp[pl.ds(j * 32 + y, 8, stride=4), :]
                    im = tmp[pl.ds((F + j) * 32 + y, 8, stride=4), :]
                    dst[at * 4 + y, 0, j, i] = re
                    dst[at * 4 + y, 1, j, i] = im - re
                    dst[at * 4 + y, 2, j, i] = im + re
            return carry

        lax.fori_loop(0, F, step, 0)

    mine = pl.multiple_of(core * 32, 32)
    by_row(low, mine, lf, core)
    by_row(upp, mine, uf, core)
    dot = functools.partial(jnp.dot, precision=HI, preferred_element_type=jnp.float32)
    for f in range(F):
        line[0, f:f + 1, :] = factor[f, 0:1, :]
        line[1, f:f + 1, :] = factor[f, 1:2, :]
    factor_re = line[0, 0:F, :]
    factor_im = line[1, 0:F, :]
    first_re = (dot(factor_re, table[0]) + dot(factor_im, table[1])) * (1.0 / 128.0)
    first_im = (dot(factor_im, table[0]) - dot(factor_re, table[1])) * (1.0 / 128.0)
    line[0, 0:F, :] = first_re
    line[1, 0:F, :] = first_im

    def build(f, carry):
        turn = lambda row: pltpu.roll(jnp.broadcast_to(row, (128, 128)), 0, 1, stride=1, stride_axis=0)
        kr = turn(line[0, pl.ds(f, 1), :])
        ki = turn(line[1, pl.ds(f, 1), :])
        for rows, cols, block in ((0, 0, kr), (0, 128, -ki), (128, 0, ki), (128, 128, kr)):
            top = block.astype(jnp.bfloat16)
            a_hi[f, rows:rows + 128, cols:cols + 128] = top
            a_lo[f, rows:rows + 128, cols:cols + 128] = (block - top.astype(jnp.float32)).astype(jnp.bfloat16)
        return carry

    lax.fori_loop(0, F, build, 0)

    forcing_out(1)
    c_copies[0].wait()
    by_row(part_l, 0, lf, other)
    c_copies[1].wait()
    by_row(part_u, 0, uf, other)

    def forward_columns(columns):
        state = [(-lf[0, 0, n], -(lf[0, 0, n] + lf[0, 1, n])) for n in columns]
        for n, v in zip(columns, state):
            pre[0, 0, n] = v[0]
            pre[0, 1, n] = v[1]

        def step(y, state):
            state = [(-w[0], -w[1]) for w in apply(lf, y, state)]
            for n, v in zip(columns, state):
                pre[y, 0, n] = v[0]
                pre[y, 1, n] = v[1]
            return state

        for n, v in zip(columns, lax.fori_loop(1, ROWS, step, state)):
            tm[0, 0, n] = v[0]
            tm[0, 1, n] = v[1]

    def forward_pair(p, carry):
        forward_columns([2 * p, 2 * p + 1])
        return carry

    lax.fori_loop(0, 2, forward_pair, 0)
    forward_columns([4])

    def r_copy(ch, to, c):
        return remote(
            send_r.at[ch, to * 2 + c], driv.at[ch, core * S + me_s], r_send.at[ch], r_recv.at[ch], to, chip * 2 + c
        )

    def r_all(ch):
        some = pl.ds(0, 2 * S - 1)
        return remote(send_r.at[ch, some], driv.at[ch, some], r_send.at[ch], r_recv.at[ch], me_s, partner)

    def r_local(ch):
        return pltpu.make_async_copy(send_r.at[ch, me_s * 2 + core], driv.at[ch, core * S + me_s], loc.at[2, ch])

    def filtered(ch, carry):
        f_local(ch).wait()
        f_all(ch).wait_recv()

        def field(f, carry):
            rhs = jnp.concatenate(
                [recv_f[ch, :, f, 0].reshape(128, 128), recv_f[ch, :, f, 1].reshape(128, 128)], axis=0
            )
            res = jnp.dot(a_hi[f], rhs, preferred_element_type=jnp.float32) + jnp.dot(
                a_lo[f], rhs, preferred_element_type=jnp.float32
            )
            re = res[:128].reshape(2 * S, 8, 128)
            im = res[128:].reshape(2 * S, 8, 128)
            top = jnp.max(jnp.maximum(jnp.abs(re), jnp.abs(im)), axis=1, keepdims=True)
            scale = jnp.maximum(top * 1.01, 1e-30).astype(jnp.bfloat16).astype(jnp.float32)
            scales[:, pl.ds(f, 1), :] = scale
            send_r[ch, :, f] = encode(re, scale).astype(jnp.bfloat16)
            send_r[ch, :, F + f] = encode(im, scale).astype(jnp.bfloat16)
            return carry

        lax.fori_loop(0, F, field, 0)
        send_r[ch, :, 2 * F] = scales[...].astype(jnp.bfloat16)
        r_local(ch).start()

        def start_r(o, carry):
            to = span_peer(o)
            r_copy(ch, to, core).start()
            r_copy(ch, to, other).start()
            return carry

        lax.fori_loop(0, S - 1, start_r, 0)
        r_copy(ch, me_s, other).start()
        return carry

    def backward_column(n, carry):
        last = ROWS - 1
        v = (-uf[last, 0, n], -(uf[last, 0, n] + uf[last, 1, n]))
        b = (pre[last, 0, n], pre[last, 1, n])

        def step(t, state):
            y = last - 1 - t
            v, b = state
            x, z = apply(uf, y, [v, b])
            return ((-x[0], -x[1]), (pre[y, 0, n] - z[0], pre[y, 1, n] - z[1]))

        v, b = lax.fori_loop(0, last, step, (v, b))
        tm[1, 0, n] = v[0]
        tm[1, 1, n] = v[1]
        tm[2, 0, n] = b[0]
        tm[2, 1, n] = b[1]
        return carry


    lax.fori_loop(0, 4, backward_column, 0)
    filtered(0, 0)
    filtered(1, 0)
    lax.fori_loop(4, F, backward_column, 0)

    def halves(p, q):
        axis = p.ndim - 1
        left = lax.broadcasted_iota(jnp.int32, p.shape, axis) < 64
        return (
            jnp.where(left, p, pltpu.roll(q, 64, axis)),
            jnp.where(left, pltpu.roll(p, 64, axis), q),
        )

    def pack_t(g, carry):
        at = g * F
        d0, d1 = halves(tm[g // F, 0, lax.rem(g, F)], tm[g // F, 1, lax.rem(g, F)])
        for i in range(F):
            send_t[pl.ds(at + i, 8, stride=TR), :] = d0[i]
            send_t[pl.ds(8 * TR + at + i, 8, stride=TR), :] = d1[i]
        return carry

    lax.fori_loop(0, 3 * F, pack_t, 0)

    def code_transfers(n, carry):
        encode_transfers(send_t, code_t, 2 * n, 2)
        return carry

    lax.fori_loop(0, K // 2, code_transfers, 0)

    def t_copy(o):
        to = wall_peer(o)
        return remote(code_t.at[to], got_t.at[chip], t_send.at[0], t_recv.at[0], me_s, to * 2 + core)

    def t_all():
        some = pl.ds(0, K - 1)
        return remote(code_t.at[some], got_t.at[some], t_send.at[0], t_recv.at[0], me_s, partner)

    t_local = pltpu.make_async_copy(code_t.at[chip], got_t.at[chip], loc.at[1, 0])
    t_local.start()

    def start_t(o, carry):
        t_copy(o).start()
        return carry

    lax.fori_loop(0, K - 1, start_t, 0)

    by_row(piv, mine, pf, core)
    c_copies[2].wait()
    by_row(part_p, 0, pf, other)

    def a_copy(ch, o):
        to = wall_peer(o)
        return remote(
            code_a.at[ch * K + to], got_a.at[ch * K + chip], a_send.at[ch], a_recv.at[ch], me_s, to * 2 + core
        )

    def a_all(ch):
        some = pl.ds(ch * K, K - 1)
        return remote(code_a.at[some], got_a.at[some], a_send.at[ch], a_recv.at[ch], me_s, partner)

    def a_local(ch):
        return pltpu.make_async_copy(code_a.at[ch * K + chip], got_a.at[ch * K + chip], loc.at[3, ch])

    zero = jnp.zeros((F, 8, 128), jnp.float32)

    def put(ref, y, state):
        for n in range(2):
            ref[y, n, 0] = state[n][0]
            ref[y, n, 1] = state[n][1]

    def get(ref, y):
        return [(ref[y, n, 0], ref[y, n, 1]) for n in range(2)]

    def local_solve(ch, carry):
        r_local(ch).wait()
        r_all(ch).wait_recv()

        def forward(y, state):
            base = (y // 4) * S + lax.rem(y, 4)
            drive = []
            for n in range(2):
                code = driv[ch, base + 4 * n].astype(jnp.float32)
                scale = jnp.stack([jnp.broadcast_to(code[2 * F, f:f + 1], (8, 128)) for f in range(F)])
                drive.append((decode(code[:F], scale), decode(code[F:2 * F], scale)))
            source = apply(pf, y, drive)
            put(src.at[ch], y, source)
            state = sub(source, apply(lf, y, state))
            put(sw, y, state)
            return state

        a = lax.fori_loop(0, ROWS, forward, [(zero, zero), (zero, zero)])

        def backward(t, state):
            y = ROWS - 2 - t
            return sub(get(sw, y), apply(uf, y, state))

        c = lax.fori_loop(0, ROWS - 1, backward, a)
        base = ch * (K * AR)
        for g, (p, q) in enumerate(((a[0][0], a[1][0]), (a[0][1], a[1][1]), (c[0][0], c[1][0]), (c[0][1], c[1][1]))):
            d0, d1 = halves(p, q)
            for i in range(F):
                send_a[pl.ds(base + g * F + i, 8, stride=AR), :] = d0[i]
                send_a[pl.ds(base + 8 * AR + g * F + i, 8, stride=AR), :] = d1[i]
        for n in range(2):
            encode_blocks(send_a, code_a, ch * K + 8 * n, 8, 1, 3, 20)
        a_local(ch).start()

        def start_a(o, carry):
            a_copy(ch, o).start()
            return carry

        lax.fori_loop(0, K - 1, start_a, 0)
        return carry

    local_solve(0, 0)

    local_solve(1, 0)

    t_local.wait()
    t_all().wait_recv()

    def plain_transfers(n, carry):
        decode_transfers(got_t, recv_t, 2 * n, 2)
        return carry

    lax.fori_loop(0, K // 2, plain_transfers, 0)

    def expand(k, carry):
        for g in range(3 * F):
            rows = recv_t[pl.ds(k * TR + g * F, F), :]
            left = lax.broadcasted_iota(jnp.int32, rows.shape, 1) < 64
            turned = pltpu.roll(rows, 64, 1)
            te[k, g // F, 0, g % F, 0:F, :] = jnp.where(left, rows, turned)
            te[k, g // F, 1, g % F, 0:F, :] = jnp.where(left, turned, rows)
        return carry

    lax.fori_loop(0, K, expand, 0)

    def small(k, m, state, start):
        re, im = start
        for j in range(F):
            tr = te[k, m, 0, j, 0:F, :]
            ti = te[k, m, 1, j, 0:F, :]
            xr = state[0][j:j + 1]
            xi = state[1][j:j + 1]
            re = re + (tr * xr - ti * xi)
            im = im + (tr * xi + ti * xr)
        return re, im

    def s_copy(ch, o):
        to = wall_peer(o)
        return remote(
            code_s.at[ch * K + to], got_s.at[ch * K + chip], s_send.at[ch], s_recv.at[ch], me_s, to * 2 + core
        )

    def s_all(ch):
        some = pl.ds(ch * K, K - 1)
        return remote(code_s.at[some], got_s.at[some], s_send.at[ch], s_recv.at[ch], me_s, partner)

    def s_local(ch):
        return pltpu.make_async_copy(code_s.at[ch * K + chip], got_s.at[ch * K + chip], loc.at[4, ch])

    flat = jnp.zeros((F, 128), jnp.float32)

    def owner_scan(ch, carry):
        a_local(ch).wait()
        a_all(ch).wait_recv()
        for n in range(2):
            decode_blocks(got_a, recv_a, ch * K + 8 * n, 8, 1, 3)

        def forward(k, state):
            base = (ch * K + k) * AR
            send_s[pl.ds(base, F), :] = state[0]
            send_s[pl.ds(base + F, F), :] = state[1]
            a = (recv_a[pl.ds(base, F), :], recv_a[pl.ds(base + F, F), :])
            c = (recv_a[pl.ds(base + 2 * F, F), :], recv_a[pl.ds(base + 3 * F, F), :])
            q = small(k, 2, state, c)
            qb[k, 0, 0:F, :] = q[0]
            qb[k, 1, 0:F, :] = q[1]
            return small(k, 0, state, a)

        lax.fori_loop(0, K, forward, (flat, flat))

        def backward(t, state):
            k = K - 1 - t
            base = (ch * K + k) * AR
            send_s[pl.ds(base + 2 * F, F), :] = state[0]
            send_s[pl.ds(base + 3 * F, F), :] = state[1]
            return small(k, 1, state, (qb[k, 0, 0:F, :], qb[k, 1, 0:F, :]))

        lax.fori_loop(0, K, backward, (flat, flat))
        for n in range(2):
            encode_blocks(send_s, code_s, ch * K + 8 * n, 8, 1, 3, 20)
        s_local(ch).start()

        def start_s(o, carry):
            s_copy(ch, o).start()
            return carry

        lax.fori_loop(0, K - 1, start_s, 0)
        return carry

    lax.fori_loop(0, 2, owner_scan, 0)

    def o_copy(ch):
        return remote(
            resp.at[other, ch], out.at[:, pl.ds(2 * ch, 2), pl.ds(core * 32, 32), :],
            o_send.at[ch], o_recv.at[ch], me_s, partner,
        )

    def o_wait(ch):
        return remote(
            resp.at[other, ch], out.at[:, pl.ds(2 * ch, 2), pl.ds(other * 32, 32), :],
            o_send.at[ch], o_recv.at[ch], me_s, partner,
        )

    def o_local(ch):
        return pltpu.make_async_copy(
            resp.at[core, ch], out.at[:, pl.ds(2 * ch, 2), pl.ds(core * 32, 32), :], loc.at[5, ch]
        )

    def final(ch, carry):
        s_local(ch).wait()
        s_all(ch).wait_recv()
        for n in range(2):
            decode_blocks(got_s, recv_s, ch * K + 8 * n, 8, 1, 3)
        base = ch * (K * AR)

        def entering(g):
            e0 = jnp.stack([recv_s[pl.ds(base + g * F + i, 8, stride=AR), :] for i in range(F)])
            e1 = jnp.stack([recv_s[pl.ds(base + 8 * AR + g * F + i, 8, stride=AR), :] for i in range(F)])
            return halves(e0, e1)

        def pair(g):
            re = entering(g)
            im = entering(g + 1)
            return [(re[0], im[0]), (re[1], im[1])]

        def forward(y, state):
            state = sub(get(src.at[ch], y), apply(lf, y, state))
            put(sw, y, state)
            return state

        lax.fori_loop(0, ROWS, forward, pair(0))

        def backward(t, state):
            y = ROWS - 1 - t
            state = sub(get(sw, y), apply(uf, y, state))
            for n in range(2):
                for ri in range(2):
                    for i in range(F):
                        resp.at[y // 4, ch, ri * F + i, n][pl.ds(lax.rem(y, 4), 8, stride=4), :] = state[n][ri][i]
            return state

        lax.fori_loop(0, ROWS, backward, pair(2))
        o_local(ch).start()
        o_copy(ch).start()
        return carry

    lax.fori_loop(0, 2, final, 0)

    for ch in range(2):
        o_local(ch).wait()
        o_wait(ch).wait_recv()
        o_copy(ch).wait_send()
        f_all(ch).wait_send()
        r_all(ch).wait_send()
        a_all(ch).wait_send()
        s_all(ch).wait_send()
    t_all().wait_send()


def tables():
    n = np.arange(128)
    angle = (n[:, None] * n[None, :] % 128) * (2.0 * math.pi / 128)
    return np.stack([np.cos(angle), np.sin(angle)]).astype(np.float32)


def local(forcing, span_factor, pivot_inverse, step_lower, step_upper):
    f32, bf16 = jnp.float32, jnp.bfloat16
    dma = pltpu.SemaphoreType.DMA
    vm = pltpu.VMEM
    flat = [x.reshape(50, 64, 128) for x in (pivot_inverse, step_lower, step_upper)]
    coef = vm((ROWS, 3, F, F, 8, 128), f32)
    rows = vm((ROWS, 2, 2, F, 8, 128), f32)
    scratch = [
        vm((2 * F, 4, 64, 128), bf16), vm((F, 2, 128), f32), vm((2, 128, 128), f32),
        vm((50, 64, 128), bf16), vm((50, 64, 128), bf16), vm((50, 64, 128), bf16),
        vm((2 * F * 32, 128), f32),
        vm((2, 8, 128), f32),
        vm((2 * S, 8, 128), f32),
        vm((2, S, F, 2, 16, 128), bf16),
        vm((2, S, F, 2, 16, 128), bf16),
        vm((50, 32, 128), bf16), vm((50, 32, 128), bf16), vm((50, 32, 128), bf16),
        coef, coef, coef, vm((ROWS, 2, F, F, 8, 128), f32),
        vm((3, 2, F, F, 8, 128), f32),
        vm((F, 256, 256), bf16), vm((F, 256, 256), bf16),
        vm((2, 2 * S, 2 * F + 1, 8, 128), bf16),
        vm((2, 2 * S, 2 * F + 1, 8, 128), bf16),
        vm((K * TR, 128), f32), vm((K * TR, 128), f32),
        vm((K, 3, 2, F, 8, 128), f32),
        vm((2 * K * AR, 128), f32), vm((2 * K * AR, 128), f32),
        vm((2 * K * AR, 128), f32), vm((2 * K * AR, 128), f32),
        vm((K, TR // 8, 8, 128), bf16), vm((K, TR // 8, 8, 128), bf16),
        vm((2 * K, 3, 8, 128), bf16), vm((2 * K, 3, 8, 128), bf16),
        vm((2 * K, 3, 8, 128), bf16), vm((2 * K, 3, 8, 128), bf16),
        vm((2, ROWS, 2, 2, F, 8, 128), f32),
        rows,
        vm((K, 2, 8, 128), f32),
        vm((2, 2, 2 * F, 2, 32, 128), f32),
        dma((3,)), dma((3,)),
        dma((2,)), dma((2,)),
        dma((2,)), dma((2,)),
        dma((1,)), dma((1,)),
        dma((2,)), dma((2,)),
        dma((2,)), dma((2,)),
        dma((2,)), dma((2,)),
        dma((6, 2)),
        dma((6,)),
    ]
    out = pl.pallas_call(
        kernel,
        out_shape=jax.ShapeDtypeStruct((2 * F, 4, 64, 128), f32),
        in_specs=[pl.BlockSpec(memory_space=pltpu.HBM)] * 6,
        out_specs=pl.BlockSpec(memory_space=pl.ANY),
        scratch_shapes=scratch,
        compiler_params=pltpu.CompilerParams(
            collective_id=0, has_side_effects=True, vmem_limit_bytes=34 << 20
        ),
    )(
        *[
            pltpu.with_memory_space_constraint(x, pltpu.HBM)
            for x in (
                forcing.reshape(2 * F, 4, 64, 128),
                jnp.swapaxes(span_factor, 0, 1),
                jnp.asarray(tables()),
                *flat,
            )
        ]
    )
    return out.reshape(2, F, 4, 16, 4, 128)


def solution(mesh):
    placed = P(None, None, None, "span", "wall", None)
    return jax.shard_map(
        local,
        mesh=mesh,
        in_specs=(placed, P(), placed, placed, placed),
        out_specs=placed,
        check_vma=False,
    )
```
